32 devices in a mesh: dp: 8 (over y, x, core), tensor: 4 (over z).
Axes of the slice: x: 2, y: 2, z: 4, core: 2. Of those that a mesh axis runs over, the one named last changes fastest.
Arguments:
- block_input: bfloat16 [8, 512, 768], P('dp', 'tensor'), may hold values from -6 to 6
- segment_ids: int32 [8, 512], P('dp', 'tensor'), may hold values from 0 to 3, never falling along the last dimension, each value on 1 to 256 neighbouring positions
- w_qkv: bfloat16 [3, 768, 768], P(None, 'dp', 'tensor'), may hold values from -2.16506351 to 2.16506351
- w_out: bfloat16 [768, 768], P('tensor', 'dp'), may hold values from -0.875 to 0.875
- w_in: bfloat16 [768, 3072], P('dp', 'tensor'), may hold values from -0.21875 to 0.21875
- w_back: bfloat16 [3072, 768], P('tensor', 'dp'), may hold values from -0.21875 to 0.21875
- qv_bias: float32 [2, 768], P(None, 'tensor'), may hold values from -3 to 3
- in_bias: float32 [3072], P('tensor'), may hold values from -3 to 3
- norm_gains: float32 [2, 768], replicated, may hold values from 0.5 to 1.5
- norm_biases: float32 [4, 768], replicated, may hold values from -2 to 2
- out_cotangent: bfloat16 [8, 512, 768], P('dp', 'tensor'), may hold values from -6 to 6
Outputs:
- block_output: bfloat16 [8, 512, 768], P('dp', 'tensor')
- input_grad: float32 [8, 512, 768], P('dp', 'tensor')
- grad_qkv: float32 [3, 768, 768], P(None, 'dp', 'tensor')
- grad_out: float32 [768, 768], P('tensor', 'dp')
- grad_in: float32 [768, 3072], P('dp', 'tensor')
- grad_back: float32 [3072, 768], P('tensor', 'dp')
- grad_qv_bias: float32 [2, 768], P(None, 'tensor')
- grad_in_bias: float32 [3072], P('tensor')
- grad_gains: float32 [2, 768], replicated
- grad_biases: float32 [4, 768], replicated
The draws below stay inside these ranges and needn't reach their ends.
Inputs may be any that keep to these rules, and one draw needn't show every extreme that they name: `segment_ids`: within each sequence segment numbers never fall; a document spans at most half of 512 tokens, and one document in each sequence spans exactly that many.
All inputs are finite; a program needn't handle non-finite values.
Results may differ from the reference program's by a relative error of at most 0.0098.
Values may be sent and summed in bfloat16 or wider, within the bound.
A program may use at most 64 MiB of HBM per device.

```python
import math
import jax
import jax.numpy as jnp
import numpy as np
from jax import lax

D = 768
HEADS = 12
FF = 3072
SEQ = 512
DOCS = 4
SEQS = 8


def draw_w_qkv(key, part):
    base_key = jax.random.fold_in(key, 0)
    base = jnp.clip(jax.random.normal(base_key, (3, D, D), jnp.float32), -6.0, 6.0) / math.sqrt(D)
    return base.astype(jnp.bfloat16)


def level_of(own_key, extent, pieces, low, high):
    level = 1.0
    for axis_at, shards_of in pieces:
        heights = jax.random.uniform(jax.random.fold_in(jax.random.fold_in(own_key, 6), axis_at), (shards_of,), jnp.float32, low / len(pieces), high / len(pieces))
        level = level * jnp.repeat(jnp.exp(heights), extent[axis_at] // shards_of).reshape((-1,) + (1,) * (len(extent) - 1 - axis_at))
    return level


def profile(amount, total, bound, lean):
    portions = [(1 << 20) // math.isqrt(rank ** lean) + 1 for rank in range(2, amount + 1)]
    rest, counts = total - bound - (amount - 1), [1] * (amount - 1)
    while rest > 0:
        movable = [i for i in range(amount - 1) if counts[i] < bound]
        mass, left = sum([portions[i] for i in movable]), rest
        for i in movable:
            addition = min(bound - counts[i], max(1, left * portions[i] // mass), rest)
            counts[i] = counts[i] + addition
            rest = rest - addition
    return np.array([bound] + counts)


def uneven_parts(stream_key, count, total, limit, slope):
    if count == 2:
        one = jax.random.randint(stream_key, (), max(1, total - limit), min(limit, total - 1) + 1)
        return jnp.stack([one, total - one])
    lengths = jnp.asarray(profile(count, total, limit, slope), jnp.int32)
    twos = (count - 1) // 2
    giver, taker = lengths[1:1 + 2 * twos:2], lengths[2:2 + 2 * twos:2]
    room = jnp.minimum(giver - 1, limit - taker)
    moved = jax.random.randint(jax.random.fold_in(stream_key, 1), (twos,), 0, 1 << 20) % (room + 1)
    lengths = lengths.at[1:1 + 2 * twos:2].set(giver - moved).at[2:2 + 2 * twos:2].set(taker + moved)
    return lengths[jax.random.permutation(jax.random.fold_in(stream_key, 2), count)]


def bell_draw(key, shape, deviation, reach, pieces=(), kind=jnp.bfloat16):
    entries = deviation * jax.random.normal(key, shape, jnp.float32)
    if pieces:
        entries = entries * level_of(key, shape, pieces, -0.22, 0.18)
    return jnp.clip(entries, -reach, reach).astype(kind)


def setup_inputs(seed: int = 0) -> dict:
    streams_of = jax.random.split(jax.random.key(seed), 12)
    return {
        "block_input": bell_draw(streams_of[0], (SEQS, SEQ, D), 1.0, 6.0, ((0, 8), (1, 4))),
        "segment_ids": jax.vmap(lambda own: jnp.searchsorted(jnp.cumsum(uneven_parts(own, DOCS, SEQ, SEQ // 2, 1)), jnp.arange(SEQ), side="right"))(jax.random.split(streams_of[1], SEQS)).reshape((SEQS, SEQ)).astype(jnp.int32),
        "w_qkv": draw_w_qkv(jax.random.fold_in(streams_of[11], 71), 0),
        "w_out": bell_draw(streams_of[3], (D, D), (D // 16) ** -0.5, 0.875, ((0, 4), (1, 8))),
        "w_in": bell_draw(streams_of[4], (D, FF), D ** -0.5, 0.21875, ((0, 8), (1, 4))),
        "w_back": bell_draw(streams_of[5], (FF, D), (FF // 4) ** -0.5, 0.21875, ((0, 4), (1, 8))),
        "qv_bias": bell_draw(streams_of[6], (2, D), 0.5, 3.0, ((1, 4),), jnp.float32),
        "in_bias": bell_draw(streams_of[7], (FF,), 0.5, 3.0, ((0, 4),), jnp.float32),
        "norm_gains": jnp.clip(jax.random.uniform(streams_of[8], (2, D), jnp.float32, 0.5, 1.5), 0.5, 1.5),
        "norm_biases": bell_draw(streams_of[9], (4, D), 0.3, 2.0, (), jnp.float32),
        "out_cotangent": bell_draw(streams_of[10], (SEQS, SEQ, D), 1.0, 6.0, ((0, 8), (1, 4))),
    }


EPS = 1e-05
GELU_C = math.sqrt(2.0 / math.pi)
GELU_A = 0.044715

def normalize(residual, gain_row, offset_row):
    centered = residual - lax.optimization_barrier(jnp.mean(residual, axis=-1, keepdims=True))
    inv_std = lax.rsqrt(lax.optimization_barrier(jnp.mean(centered * centered, axis=-1, keepdims=True)) + EPS)
    normed = centered * inv_std
    return (normed * gain_row + offset_row, normed, inv_std)

def normalize_back(upstream, normed, inv_std, gain_row):
    scaled = upstream * gain_row
    return inv_std * (scaled - lax.optimization_barrier(jnp.mean(scaled, axis=-1, keepdims=True)) - normed * lax.optimization_barrier(jnp.mean(scaled * normed, axis=-1, keepdims=True)))

def gelu_pair(inputs):
    inner_arg = GELU_C * (inputs + GELU_A * inputs * inputs * inputs)
    tangent_h = jnp.tanh(inner_arg)
    value_out = 0.5 * inputs * (1.0 + tangent_h)
    slope_out = 0.5 * (1.0 + tangent_h) + 0.5 * inputs * (1.0 - tangent_h * tangent_h) * GELU_C * (1.0 + 3.0 * GELU_A * inputs * inputs)
    return (value_out, slope_out)

def masked_scores(query_block, key_rows, segment, row_start, key_end, num_heads):
    block_rows = query_block.shape[0]
    width = query_block.shape[1] // num_heads
    query_heads = query_block.reshape(block_rows, num_heads, width).astype(jnp.float32)
    key_heads = key_rows[:key_end].reshape(key_end, num_heads, width).astype(jnp.float32)
    raw_scores = jnp.einsum('qhd,khd->hqk', query_heads, key_heads) * (1.0 / math.sqrt(width))
    query_pos = row_start + jnp.arange(block_rows, dtype=jnp.int32)
    key_pos = jnp.arange(key_end, dtype=jnp.int32)
    allowed = (key_pos[None, :] <= query_pos[:, None]) & (segment[:key_end][None, :] == segment[row_start:key_end][:, None])
    return jnp.where(allowed[None], raw_scores, -jnp.inf)

def attend_forward(queries, key_rows, values, segment, num_heads):
    total_rows = queries.shape[0]
    block_rows = min(512, total_rows)
    width = queries.shape[1] // num_heads
    contexts = []
    totals = []
    for block_index in range(total_rows // block_rows):
        row_start = block_index * block_rows
        key_end = row_start + block_rows
        scores = masked_scores(queries[row_start:key_end], key_rows, segment, row_start, key_end, num_heads)
        row_max = lax.optimization_barrier(jnp.max(scores, axis=-1, keepdims=True))
        log_total = row_max + jnp.log(lax.optimization_barrier(jnp.sum(jnp.exp(scores - row_max), axis=-1, keepdims=True)))
        weights = jnp.exp(scores - log_total).astype(jnp.bfloat16)
        value_heads = values[:key_end].reshape(key_end, num_heads, width)
        context = jnp.einsum('hqk,khd->qhd', weights.astype(jnp.float32), value_heads.astype(jnp.float32))
        contexts.append(context.reshape(block_rows, num_heads * width).astype(jnp.bfloat16))
        totals.append(log_total)
    return (jnp.concatenate(contexts, axis=0), jnp.concatenate(totals, axis=1))

def attend_backward(queries, key_rows, values, segment, context, log_total, context_grad, num_heads):
    total_rows = queries.shape[0]
    block_rows = min(512, total_rows)
    width = queries.shape[1] // num_heads
    inv_root = 1.0 / math.sqrt(width)
    query_grads = []
    key_grad = jnp.zeros((total_rows, num_heads, width), jnp.float32)
    value_grad = jnp.zeros((total_rows, num_heads, width), jnp.float32)
    for block_index in range(total_rows // block_rows):
        row_start = block_index * block_rows
        key_end = row_start + block_rows
        scores = masked_scores(queries[row_start:key_end], key_rows, segment, row_start, key_end, num_heads)
        probs = jnp.exp(scores - log_total[:, row_start:key_end])
        probs_half = probs.astype(jnp.bfloat16)
        grad_heads = context_grad[row_start:key_end].reshape(block_rows, num_heads, width).astype(jnp.float32)
        context_heads = context[row_start:key_end].reshape(block_rows, num_heads, width).astype(jnp.float32)
        value_heads = values[:key_end].reshape(key_end, num_heads, width).astype(jnp.float32)
        key_heads = key_rows[:key_end].reshape(key_end, num_heads, width).astype(jnp.float32)
        query_heads = queries[row_start:key_end].reshape(block_rows, num_heads, width).astype(jnp.float32)
        prob_grad = jnp.einsum('qhd,khd->hqk', grad_heads, value_heads)
        row_dot = jnp.transpose(lax.optimization_barrier(jnp.sum(grad_heads * context_heads, axis=-1)))[:, :, None]
        score_grad = (probs * (prob_grad - row_dot) * inv_root).astype(jnp.bfloat16).astype(jnp.float32)
        query_grads.append(jnp.einsum('hqk,khd->qhd', score_grad, key_heads).reshape(block_rows, num_heads * width))
        key_grad = key_grad.at[:key_end].add(jnp.einsum('hqk,qhd->khd', score_grad, query_heads))
        value_grad = value_grad.at[:key_end].add(jnp.einsum('hqk,qhd->khd', probs_half.astype(jnp.float32), grad_heads))
    return (jnp.concatenate(query_grads, axis=0), key_grad.reshape(total_rows, num_heads * width), value_grad.reshape(total_rows, num_heads * width))

def reference(block_input, segment_ids, w_qkv, w_out, w_in, w_back, qv_bias, in_bias, norm_gains, norm_biases, out_cotangent):

    def one_sequence(totals, sequence_item):
        inputs, segment, cotangent_half = sequence_item
        residual = inputs.astype(jnp.float32)
        first_out, normed_first, inv_first = normalize(residual, norm_gains[0], norm_biases[0])
        first_half = first_out.astype(jnp.bfloat16)
        projected = jnp.einsum('sd,cde->sce', first_half.astype(jnp.float32), w_qkv.astype(jnp.float32))
        queries = (projected[:, 0] + qv_bias[0]).astype(jnp.bfloat16)
        key_rows = projected[:, 1].astype(jnp.bfloat16)
        values = (projected[:, 2] + qv_bias[1]).astype(jnp.bfloat16)
        context, log_total = attend_forward(queries, key_rows, values, segment, HEADS)
        middle = residual + jnp.dot(context, w_out, preferred_element_type=jnp.float32) + norm_biases[2]
        second_out, normed_second, inv_second = normalize(middle, norm_gains[1], norm_biases[1])
        second_half = second_out.astype(jnp.bfloat16)
        hidden_pre = jnp.dot(second_half, w_in, preferred_element_type=jnp.float32) + in_bias
        gelu_value, gelu_slope = gelu_pair(hidden_pre)
        activation = gelu_value.astype(jnp.bfloat16)
        output_full = middle + jnp.dot(activation, w_back, preferred_element_type=jnp.float32) + norm_biases[3]
        block_out = output_full.astype(jnp.bfloat16)
        cotangent = cotangent_half.astype(jnp.float32)
        grad_back_part = jnp.dot(activation.T, cotangent_half, preferred_element_type=jnp.float32)
        hidden_grad = jnp.dot(cotangent_half, w_back.T, preferred_element_type=jnp.float32) * gelu_slope
        hidden_half = hidden_grad.astype(jnp.bfloat16)
        grad_in_part = jnp.dot(second_half.T, hidden_half, preferred_element_type=jnp.float32)
        second_grad = jnp.dot(hidden_half, w_in.T, preferred_element_type=jnp.float32)
        middle_grad = cotangent + normalize_back(second_grad, normed_second, inv_second, norm_gains[1])
        middle_half = middle_grad.astype(jnp.bfloat16)
        grad_out_part = jnp.dot(context.T, middle_half, preferred_element_type=jnp.float32)
        context_grad = jnp.dot(middle_half, w_out.T, preferred_element_type=jnp.float32).astype(jnp.bfloat16)
        query_grad, key_grad, value_grad = attend_backward(queries, key_rows, values, segment, context, log_total, context_grad, HEADS)
        proj_half = jnp.stack([query_grad, key_grad, value_grad], axis=1).astype(jnp.bfloat16).astype(jnp.float32)
        grad_qkv_part = jnp.einsum('sd,sce->cde', first_half.astype(jnp.float32), proj_half)
        first_grad = jnp.einsum('sce,cde->sd', proj_half, w_qkv.astype(jnp.float32))
        input_grad = middle_grad + normalize_back(first_grad, normed_first, inv_first, norm_gains[0])
        parts = (grad_qkv_part, grad_out_part, grad_in_part, grad_back_part, jnp.stack([lax.optimization_barrier(jnp.sum(query_grad, axis=0)), lax.optimization_barrier(jnp.sum(value_grad, axis=0))]), lax.optimization_barrier(jnp.sum(hidden_grad, axis=0)), jnp.stack([lax.optimization_barrier(jnp.sum(first_grad * normed_first, axis=0)), lax.optimization_barrier(jnp.sum(second_grad * normed_second, axis=0))]), jnp.stack([lax.optimization_barrier(jnp.sum(first_grad, axis=0)), lax.optimization_barrier(jnp.sum(second_grad, axis=0)), lax.optimization_barrier(jnp.sum(middle_grad, axis=0)), lax.optimization_barrier(jnp.sum(cotangent, axis=0))]))
        new_totals = tuple((total + part for total, part in zip(totals, parts)))
        return (new_totals, (block_out, input_grad))
    initial = (jnp.zeros((3, D, D), jnp.float32), jnp.zeros((D, D), jnp.float32), jnp.zeros((D, FF), jnp.float32), jnp.zeros((FF, D), jnp.float32), jnp.zeros((2, D), jnp.float32), jnp.zeros((FF,), jnp.float32), jnp.zeros((2, D), jnp.float32), jnp.zeros((4, D), jnp.float32))
    totals, (outputs, grads) = lax.scan(one_sequence, initial, (block_input, segment_ids, out_cotangent))
    return (outputs, grads, totals[0], totals[1], totals[2], totals[3], totals[4], totals[5], totals[6], totals[7])
```

```python
import functools
import math

import jax
import jax.numpy as jnp
from jax import lax
from jax.experimental import pallas as pl
from jax.experimental.pallas import tpu as pltpu
from jax.sharding import PartitionSpec as P

HEAD = 64


EPS = 1e-05
GELU_C = math.sqrt(2.0 / math.pi)
GELU_A = 0.044715


def normalize(residual, gain_row, offset_row):
    centered = residual - jnp.mean(residual, axis=-1, keepdims=True)
    inv_std = lax.rsqrt(jnp.mean(centered * centered, axis=-1, keepdims=True) + EPS)
    normed = centered * inv_std
    return (normed * gain_row + offset_row, normed, inv_std)


def normalize_back(upstream, normed, inv_std, gain_row):
    scaled = upstream * gain_row
    return inv_std * (
        scaled
        - jnp.mean(scaled, axis=-1, keepdims=True)
        - normed * jnp.mean(scaled * normed, axis=-1, keepdims=True)
    )


def gelu_pair(inputs):
    inner_arg = GELU_C * (inputs + GELU_A * inputs * inputs * inputs)
    tangent_h = jnp.tanh(inner_arg)
    value_out = 0.5 * inputs * (1.0 + tangent_h)
    slope_out = 0.5 * (1.0 + tangent_h) + 0.5 * inputs * (1.0 - tangent_h * tangent_h) * GELU_C * (
        1.0 + 3.0 * GELU_A * inputs * inputs
    )
    return (value_out, slope_out)


def contract_rows(left, right):
    return lax.dot_general(
        left, right, (((0,), (0,)), ((), ())), preferred_element_type=jnp.float32
    )


def contract_cols(left, right):
    return lax.dot_general(
        left, right, (((1,), (1,)), ((), ())), preferred_element_type=jnp.float32
    )


def masked_scores(query_block, key_rows, segment, key_end, num_heads):
    block_rows = query_block.shape[0]
    width = query_block.shape[1] // num_heads
    query_heads = query_block.reshape(block_rows, num_heads, width)
    key_heads = key_rows.reshape(key_end, num_heads, width)
    raw_scores = jnp.einsum(
        "qhd,khd->hqk", query_heads, key_heads, preferred_element_type=jnp.float32
    ) * (1.0 / math.sqrt(width))
    query_pos = jnp.arange(block_rows, dtype=jnp.int32)
    key_pos = jnp.arange(key_end, dtype=jnp.int32)
    allowed = (key_pos[None, :] <= query_pos[:, None]) & (segment[None, :] == segment[:, None])
    return jnp.where(allowed[None], raw_scores, -jnp.inf)


def attend_forward(queries, key_rows, values, segment, num_heads):
    total_rows = queries.shape[0]
    block_rows = min(512, total_rows)
    width = queries.shape[1] // num_heads
    scores = masked_scores(queries, key_rows, segment, block_rows, num_heads)
    row_max = jnp.max(scores, axis=-1, keepdims=True)
    log_total = row_max + jnp.log(jnp.sum(jnp.exp(scores - row_max), axis=-1, keepdims=True))
    weights = jnp.exp(scores - log_total).astype(jnp.bfloat16)
    value_heads = values.reshape(block_rows, num_heads, width)
    context = jnp.einsum("hqk,khd->qhd", weights, value_heads, preferred_element_type=jnp.float32)
    contexts = context.reshape(block_rows, num_heads * width).astype(jnp.bfloat16)
    return (contexts, log_total)


def attend_backward(
    queries, key_rows, values, segment, context, log_total, context_grad, num_heads
):
    total_rows = queries.shape[0]
    block_rows = min(512, total_rows)
    width = queries.shape[1] // num_heads
    inv_root = 1.0 / math.sqrt(width)
    key_grad = jnp.zeros((total_rows, num_heads, width), jnp.float32)
    value_grad = jnp.zeros((total_rows, num_heads, width), jnp.float32)
    scores = masked_scores(queries, key_rows, segment, block_rows, num_heads)
    probs = jnp.exp(scores - log_total)
    probs_half = probs.astype(jnp.bfloat16)
    grad_heads = context_grad.reshape(block_rows, num_heads, width)
    context_heads = context.reshape(block_rows, num_heads, width)
    value_heads = values.reshape(block_rows, num_heads, width)
    key_heads = key_rows.reshape(block_rows, num_heads, width)
    query_heads = queries.reshape(block_rows, num_heads, width)
    prob_grad = jnp.einsum(
        "qhd,khd->hqk", grad_heads, value_heads, preferred_element_type=jnp.float32
    )
    row_dot = jnp.transpose(
        jnp.sum(grad_heads.astype(jnp.float32) * context_heads.astype(jnp.float32), axis=-1)
    )[:, :, None]
    score_grad = (probs * (prob_grad - row_dot) * inv_root).astype(jnp.bfloat16)
    query_grads = jnp.einsum(
        "hqk,khd->qhd", score_grad, key_heads, preferred_element_type=jnp.float32
    ).reshape(block_rows, num_heads * width)
    key_grad = key_grad.at[:block_rows].add(
        jnp.einsum("hqk,qhd->khd", score_grad, query_heads, preferred_element_type=jnp.float32)
    )
    value_grad = value_grad.at[:block_rows].add(
        jnp.einsum("hqk,qhd->khd", probs_half, grad_heads, preferred_element_type=jnp.float32)
    )
    return (
        query_grads,
        key_grad.reshape(total_rows, num_heads * width),
        value_grad.reshape(total_rows, num_heads * width),
    )


def half_scatter(share):
    return lax.psum_scatter(
        share.astype(jnp.bfloat16), "tensor", scatter_dimension=0, tiled=True
    ).astype(jnp.float32)


def shards(
    block_input,
    segment_ids,
    w_qkv,
    w_out,
    w_in,
    w_back,
    qv_bias,
    in_bias,
    norm_gains,
    norm_biases,
    out_cotangent,
):
    bf16 = jnp.bfloat16
    residual = block_input[0].astype(jnp.float32)
    head_cols = w_qkv.shape[2]
    hidden_cols = w_in.shape[1]
    local_heads = head_cols // HEAD
    cuts = [head_cols, 2 * head_cols, 3 * head_cols, 4 * head_cols, 4 * head_cols + hidden_cols]
    packed = jnp.concatenate([w_qkv[0], w_qkv[1], w_qkv[2], w_out.T, w_in, w_back.T], axis=1)
    full = lax.all_gather(packed, "dp", axis=0, tiled=True)
    qkv_full = full[:, : cuts[2]]
    out_full = full[:, cuts[2] : cuts[3]]
    in_full = full[:, cuts[3] : cuts[4]]
    back_full = full[:, cuts[4] :]
    first_out, normed_first, inv_first = normalize(residual, norm_gains[0], norm_biases[0])
    first_half, segment, cotangent_full = (
        lax.all_gather(first_out.astype(bf16), "tensor", axis=0, tiled=True),
        lax.all_gather(segment_ids[0], "tensor", axis=0, tiled=True),
        lax.all_gather(out_cotangent[0], "tensor", axis=0, tiled=True),
    )
    projected = jnp.dot(first_half, qkv_full, preferred_element_type=jnp.float32)
    queries = (projected[:, : cuts[0]] + qv_bias[0]).astype(bf16)
    key_rows = projected[:, cuts[0] : cuts[1]].astype(bf16)
    values = (projected[:, cuts[1] :] + qv_bias[1]).astype(bf16)
    context, log_total = attend_forward(queries, key_rows, values, segment, local_heads)
    attn_share = half_scatter(contract_cols(context, out_full))
    middle = residual + attn_share + norm_biases[2]
    second_out, normed_second, inv_second = normalize(middle, norm_gains[1], norm_biases[1])
    second_half = lax.all_gather(second_out.astype(bf16), "tensor", axis=0, tiled=True)
    hidden_pre = jnp.dot(second_half, in_full, preferred_element_type=jnp.float32) + in_bias
    gelu_value, gelu_slope = gelu_pair(hidden_pre)
    activation = gelu_value.astype(bf16)
    mlp_share = half_scatter(contract_cols(activation, back_full))
    block_out = (middle + mlp_share + norm_biases[3]).astype(bf16)
    cotangent = out_cotangent[0].astype(jnp.float32)
    grad_back_part = contract_rows(cotangent_full, activation)
    hidden_grad = jnp.dot(cotangent_full, back_full, preferred_element_type=jnp.float32) * gelu_slope
    hidden_half = hidden_grad.astype(bf16)
    grad_in_part = contract_rows(second_half, hidden_half)
    second_grad = half_scatter(contract_cols(hidden_half, in_full))
    middle_grad = cotangent + normalize_back(second_grad, normed_second, inv_second, norm_gains[1])
    middle_full = lax.all_gather(middle_grad.astype(bf16), "tensor", axis=0, tiled=True)
    grad_out_part = contract_rows(middle_full, context)
    context_grad = jnp.dot(middle_full, out_full, preferred_element_type=jnp.float32).astype(bf16)
    query_grad, key_grad, value_grad = attend_backward(
        queries, key_rows, values, segment, context, log_total, context_grad, local_heads
    )
    proj_half = jnp.concatenate([query_grad, key_grad, value_grad], axis=1).astype(bf16)
    grad_qkv_part = contract_rows(first_half, proj_half)
    first_grad = half_scatter(contract_cols(proj_half, qkv_full))
    input_grad = middle_grad + normalize_back(first_grad, normed_first, inv_first, norm_gains[0])
    parts = jnp.concatenate(
        [grad_qkv_part, grad_out_part, grad_in_part, grad_back_part], axis=1
    ).astype(bf16)
    grads = lax.psum_scatter(parts, "dp", scatter_dimension=0, tiled=True).astype(jnp.float32)
    grad_qkv = jnp.stack([grads[:, : cuts[0]], grads[:, cuts[0] : cuts[1]], grads[:, cuts[1] : cuts[2]]])
    grad_out = grads[:, cuts[2] : cuts[3]].T
    grad_in = grads[:, cuts[3] : cuts[4]]
    grad_back = grads[:, cuts[4] :].T
    own = jnp.concatenate(
        [jnp.sum(query_grad, axis=0), jnp.sum(value_grad, axis=0), jnp.sum(hidden_grad, axis=0)]
    )
    tensors = lax.axis_size("tensor")
    rank = lax.axis_index("tensor")
    spread = jnp.where(jnp.arange(tensors)[:, None] == rank, own[None], 0.0)
    norm_terms = jnp.stack(
        [
            jnp.sum(first_grad * normed_first, axis=0),
            jnp.sum(second_grad * normed_second, axis=0),
            jnp.sum(first_grad, axis=0),
            jnp.sum(second_grad, axis=0),
            jnp.sum(middle_grad, axis=0),
            jnp.sum(cotangent, axis=0),
        ]
    )
    total = lax.psum(
        jnp.concatenate([spread.reshape(-1), norm_terms.reshape(-1)]), ("dp", "tensor")
    )
    width = own.shape[0]
    own_total = lax.dynamic_slice(total, (rank * width,), (width,))
    norm_total = total[tensors * width :].reshape(norm_terms.shape)
    return (
        block_out[None],
        input_grad[None],
        grad_qkv,
        grad_out,
        grad_in,
        grad_back,
        own_total[: 2 * head_cols].reshape(2, head_cols),
        own_total[2 * head_cols :],
        norm_total[:2],
        norm_total[2:],
    )


def matmul(left, right):
    return jnp.dot(left, right, preferred_element_type=jnp.float32)


def layer_kernel(
    nt,
    nd,
    x_ref,
    seg_ref,
    wq_ref,
    wo_ref,
    wi_ref,
    wb_ref,
    cot_ref,
    qvb_ref,
    inb_ref,
    gains_ref,
    biases_ref,
    bo_ref,
    ig_ref,
    gq_ref,
    go_ref,
    gi_ref,
    gb_ref,
    gqv_ref,
    ginb_ref,
    ggain_ref,
    gbias_ref,
    fq,
    fo,
    own_out,
    fw,
    first_ref,
    second_g,
    cot_g,
    midb,
    segs,
    qs,
    ks,
    vs,
    ctx,
    ctx_all,
    call,
    cgs,
    cg,
    probs,
    hb,
    act,
    hh,
    ph,
    kacc,
    vacc,
    fsend,
    frecv,
    shares,
    share_out,
    share_in,
    mid,
    norm1,
    norm2,
    mgrad,
    fown,
    pw,
    rw,
    wz,
    wzr,
    wsum,
    wx,
    pq,
    aq,
    bq,
    rq,
    oq,
    po,
    ao,
    bo,
    ro,
    ozw,
    oz,
    ozs,
    ozt,
    inbs,
    hsum,
    hrecv,
    small,
    zsmall,
    psmall,
    csmall,
    gs,
    gr,
    ss,
    rs,
):
    bf16 = jnp.bfloat16
    f32 = jnp.float32
    nc = nd // 2
    t = lax.axis_index("tensor")
    d = lax.axis_index("dp")
    core = lax.rem(d, 2)
    chip = d // 2
    T, D = x_ref.shape
    rows = wi_ref.shape[0]
    E = ctx.shape[1]
    F = wi_ref.shape[1]
    half = F // 2
    heads = E // HEAD
    seq = nt * T
    cy, cx = chip // 2, lax.rem(chip, 2)
    chips = (chip, cy * 2 + 1 - cx, (1 - cy) * 2 + cx, (1 - cy) * 2 + 1 - cx)
    partner = {"dp": chip * 2 + 1 - core}
    along = [{"dp": c * 2 + core} for c in chips]
    near = {"tensor": t + 1 - 2 * lax.rem(t, 2)}
    far = {"tensor": lax.rem(t + 2, nt)}

    def remote(src, dst, ssem, rsem, where):
        return pltpu.make_async_remote_copy(
            src_ref=src,
            dst_ref=dst,
            send_sem=ssem,
            recv_sem=rsem,
            device_id=where,
            device_id_type=pl.DeviceIdType.MESH,
        )

    used = []
    sent = []

    def slot(count=1):
        used.extend([0] * count)
        return len(used) - count

    def link(src, dst, where):
        i = slot()
        copy = remote(src, dst, ss.at[i], rs.at[i], where)
        copy.start()
        sent.append(copy)
        return copy

    def link_all(piece, places):
        return [link(piece, piece, where) for where in places]

    def blk(index, size=T):
        return pl.ds(pl.multiple_of(index * size, size), size)

    def chip_rows(k):
        return blk(chips[k], 2 * rows)

    def core_rows(k, c):
        return blk(chips[k] * 2 + c, rows)

    def other(k):
        return lax.rem(t + k, nt)

    def line_copy(kind, place, ref, b, to):
        piece = ref.at[blk(b)]
        return remote(piece, piece, gs.at[kind, place], gr.at[kind, b], {"tensor": to})

    def line_own(kind, ref, act_on):
        for place, to in ((0, t + 1), (2 * nt - 1, t - 1)):

            @pl.when((to >= 0) & (to < nt))
            def _():
                act_on(line_copy(kind, place, ref, t, to))

    def line_place(s):
        sign = 2 * (s % 2) - 1
        return t + sign * ((s + 1) // 2), t - sign

    def gather_send(kind, ref):
        line_own(kind, ref, lambda copy: copy.start())

    def gather_step(kind, ref, s):
        b, to = line_place(s)

        @pl.when((b >= 0) & (b < nt))
        def _():
            remote(
                ref.at[blk(b)], ref.at[blk(b)], gs.at[kind, 0], gr.at[kind, b], {"tensor": b}
            ).wait_recv()

            @pl.when((to >= 0) & (to < nt))
            def _():
                line_copy(kind, s, ref, b, to).start()

    def gather_drain(kind, ref):
        line_own(kind, ref, lambda copy: copy.wait_send())

        for s in range(1, 2 * nt - 1):
            b, to = line_place(s)

            @pl.when((b >= 0) & (b < nt) & (to >= 0) & (to < nt))
            def _():
                line_copy(kind, s, ref, b, to).wait_send()

    barrier = pltpu.get_barrier_semaphore()
    for where in [{"tensor": other(k)} for k in range(1, nt)] + along[1:] + [partner]:
        pl.semaphore_signal(barrier, inc=1, device_id=where, device_id_type=pl.DeviceIdType.MESH)
    residual = x_ref[...].astype(f32)
    first_out, normed_first, inv_first = normalize(residual, gains_ref[0:1], biases_ref[0:1])
    norm1[...] = normed_first
    first_ref[blk(t), :] = first_out.astype(bf16)
    fq[blk(d, rows), :] = jnp.concatenate([wq_ref[0], wq_ref[1], wq_ref[2]], axis=1)
    own_out[t] = jnp.transpose(wo_ref[...].astype(f32)).astype(bf16)
    mine, theirs = blk(core, half), blk(1 - core, half)
    fw[0, blk(d, rows), :half] = wi_ref[:, mine]
    fw[1, blk(d, rows), :half] = wb_ref[:, mine]
    segs[t] = jnp.broadcast_to(seg_ref[...], segs.shape[1:])
    inbs[0] = jnp.broadcast_to(inb_ref[:, mine], inbs.shape[1:])
    pl.semaphore_wait(barrier, nt - 1 + nc - 1 + 1)

    gather_send(0, first_ref)
    own_rows = blk(d, rows)
    lines = [{"tensor": other(k)} for k in range(1, nt)]
    q_piece = fq.at[own_rows]
    q_in = link_all(q_piece, along[1:])
    w_pair = [
        link(ref.at[:, theirs], fw.at[w, own_rows, pl.ds(0, half)], partner)
        for w, ref in ((0, wi_ref), (1, wb_ref))
    ]
    q_pair = link_all(q_piece, [partner])
    seg_in = link_all(segs.at[t], lines)
    cot_pair = link(cot_ref, cot_g.at[pl.ds(T, T)], partner)
    cot_g[0:T] = cot_ref[...]

    w_in = {}

    def w_send(part, w, n=1):
        piece = fw.at[pl.ds(w, n), chip_rows(0), pl.ds(part * half, half)]
        w_in[part, w, 1], w_in[part, w, 2] = link_all(piece, along[1:3])

    def w_forward(part, w, n=1):
        cols = pl.ds(part * half, half)
        w_in[part, w, 1].wait_recv()
        piece = fw.at[pl.ds(w, n), core_rows(1, 0), cols]
        w_in[part, w, 3] = link(piece, piece, along[2])
        w_in[part, w, 2].wait_recv()
        piece = fw.at[pl.ds(w, n), core_rows(2, 1), cols]
        w_in[part, w, 4] = link(piece, piece, along[1])

    def w_wait(part, w):
        w_in[part, w, 3].wait_recv()
        w_in[part, w, 4].wait_recv()

    for copy in w_pair:
        copy.wait_recv()
    w_send(0, 0, 2)
    gather_step(0, first_ref, 1)
    gather_step(0, first_ref, 2)
    o_line = [link(own_out.at[t], own_out.at[t], where) for where in lines]
    w_far = [
        link(
            fw.at[w, chip_rows(0), pl.ds(0, half)], fw.at[w, chip_rows(0), pl.ds(half, half)], far
        )
        for w in (1, 0)
    ]
    inb_far = link(inbs.at[0], inbs.at[1], far)
    for k in (1, 2, 3):
        q_in[k - 1].wait_recv()
        q_pair += link_all(fq.at[core_rows(k, core)], [partner])
    gather_step(0, first_ref, 3)
    gather_step(0, first_ref, 4)
    for copy in o_line:
        copy.wait_recv()
    fo[own_rows, :] = jnp.concatenate([own_out[j] for j in range(nt)], axis=1)
    o_pair = link_all(fo.at[own_rows], [partner])
    o_in = link_all(fo.at[own_rows], along[1:])
    w_forward(0, 0, 2)
    for s in range(5, 2 * nt - 1):
        gather_step(0, first_ref, s)
    cot_near = link(cot_ref, cot_g.at[pl.ds(2 * T, T)], near)
    for copy in q_pair:
        copy.wait_recv()

    inv_root = 1.0 / math.sqrt(HEAD)
    projected = matmul(first_ref[...], fq[...])
    qs[...] = (projected[:, :E] + qvb_ref[0:1]).astype(bf16)
    ks[...] = projected[:, E : 2 * E].astype(bf16)
    vs[...] = (projected[:, 2 * E :] + qvb_ref[1:2]).astype(bf16)
    for copy in seg_in:
        copy.wait_recv()

    reach = (seq // 2 - 1 + T - 1) // T
    a2a = slot(2 * nt)
    for b in range(nt):
        low = max(0, b - reach)
        width = (b + 1 - low) * T
        key_seg = jnp.concatenate([segs[j][0:1].astype(f32) for j in range(low, b + 1)], axis=1)
        query_seg = jnp.transpose(jnp.broadcast_to(segs[b][0:1].astype(f32), (T, T)))[:, 0:1]
        query_pos = lax.broadcasted_iota(jnp.int32, (T, width), 0) + b * T
        key_pos = lax.broadcasted_iota(jnp.int32, (T, width), 1) + low * T
        allowed = (key_pos <= query_pos) & (query_seg == key_seg)
        for h in range(heads):
            cols = slice(h * HEAD, (h + 1) * HEAD)
            scores = (
                contract_cols(qs[b * T : (b + 1) * T, cols], ks[low * T : (b + 1) * T, cols])
                * inv_root
            )
            scores = jnp.where(allowed, scores, -jnp.inf)
            row_max = jnp.max(scores, axis=-1, keepdims=True)
            powers = jnp.exp(scores - row_max)
            prob = powers * (1.0 / jnp.sum(powers, axis=-1, keepdims=True))
            probs[h, b, :, :width] = prob
            ctx[b * T : (b + 1) * T, cols] = matmul(
                prob.astype(bf16), vs[low * T : (b + 1) * T, cols]
            ).astype(bf16)

        @pl.when(t == b)
        def _():
            ctx_all[t] = ctx[b * T : (b + 1) * T, :]

        @pl.when(t != b)
        def _():
            remote(
                ctx.at[pl.ds(b * T, T)], ctx_all.at[t], ss.at[a2a + b], rs.at[a2a + t], {"tensor": b}
            ).start()

    for k in (1, 2, 3):
        o_in[k - 1].wait_recv()
        o_pair += link_all(fo.at[core_rows(k, core)], [partner])
    for n, w in enumerate((1, 0)):
        w_far[n].wait_recv()
        w_send(1, w)
    for k in range(1, nt):
        src = other(k)
        remote(ctx_all.at[src], ctx_all.at[src], ss.at[a2a], rs.at[a2a + src], far).wait_recv()
    call[...] = jnp.concatenate([ctx_all[j] for j in range(nt)], axis=1)
    for copy in o_pair:
        copy.wait_recv()
    middle = residual + contract_cols(call[...], fo[...]) + biases_ref[2:3]
    mid[...] = middle
    second_out, normed_second, inv_second = normalize(middle, gains_ref[1:2], biases_ref[1:2])
    norm2[...] = normed_second
    second_g[0:T] = second_out.astype(bf16)
    second_piece = second_g.at[pl.ds(0, T)]
    s_near = link(second_piece, second_g.at[pl.ds(2 * T, T)], near)
    s_pair = link(second_piece, second_g.at[pl.ds(T, T)], partner)
    w_forward(1, 1)
    w_wait(0, 0)
    inb_far.wait_recv()
    cot_near.wait_recv()
    cot_pair2 = link(cot_g.at[pl.ds(2 * T, T)], cot_g.at[pl.ds(3 * T, T)], partner)
    cot_pair.wait_recv()

    def member(s):
        return slice(s * T, (s + 1) * T)

    def back(s):
        hb[member(s), :] = matmul(cot_g[member(s), :], fw[1])

    hidden_bias = jnp.concatenate([inbs[0][0:1], inbs[1][0:1]], axis=1)
    small[...] = jnp.zeros_like(small)

    def hidden(s):
        pre = matmul(second_g[member(s), :], fw[0]) + hidden_bias
        value, slope = gelu_pair(pre)
        act[member(s), :] = value.astype(bf16)
        grad = hb[member(s), :] * slope
        total = jnp.sum(grad, axis=0, keepdims=True)
        if s == 0:
            hsum[...] = jnp.broadcast_to(total, hsum.shape)
        else:
            hsum[...] += total
        hh[member(s), :] = grad.astype(bf16)

    group = {}

    def share(n, s, value):
        if s % 2 == 0:
            shares[n, s // 2] = value
            return
        share_out[n, s // 2] = value.astype(bf16)
        group[n, s] = link(share_out.at[n, s // 2], share_in.at[n, s // 2], partner)

    def share_near(n):
        group[n, 3].wait_recv()
        share_out[n, 2] = (shares[n, 1] + share_in[n, 1].astype(f32)).astype(bf16)
        group[n, 4] = link(share_out.at[n, 2], share_in.at[n, 2], near)

    def share_total(n):
        group[n, 1].wait_recv()
        group[n, 4].wait_recv()
        return shares[n, 0] + share_in[n, 0].astype(f32) + share_in[n, 2].astype(f32)

    w_forward(1, 0)
    w_wait(1, 1)
    back(0)
    back(1)
    w_wait(1, 0)
    hidden(0)
    share(0, 0, contract_cols(hh[member(0), :], fw[0]))
    s_pair.wait_recv()
    hidden(1)
    share(0, 1, contract_cols(hh[member(1), :], fw[0]))
    back(2)
    s_near.wait_recv()
    s_pair2 = link(second_g.at[pl.ds(2 * T, T)], second_g.at[pl.ds(3 * T, T)], partner)
    hidden(2)
    share(0, 2, contract_cols(hh[member(2), :], fw[0]))
    cot_pair2.wait_recv()
    back(3)
    s_pair2.wait_recv()
    hidden(3)
    share(0, 3, contract_cols(hh[member(3), :], fw[0]))
    share_near(0)
    h_far = link(hsum.at[:, pl.ds(half, half)], hrecv, far)

    step = 128

    def grad_rows(w, left, right):
        def chunk(c, carry):
            pw[w, blk(c, step), :] = contract_rows(left[:, blk(c, step)], right[...]).astype(bf16)
            return carry

        lax.fori_loop(0, D // step, chunk, 0)

    wg = {}

    def w_grads(part, w, n=1):
        cols = pl.ds(part * half, half)
        for k in (1, 2, 3):
            wg[part, w, k] = link(
                pw.at[pl.ds(w, n), chip_rows(k), cols],
                rw.at[part, k - 1, pl.ds(w, n)],
                along[k],
            )

    def w_sum(part, ws):
        for w in ws:
            for k in (1, 2, 3):
                wg[part, w, k].wait_recv()
        total = pw[:, chip_rows(0), part * half : (part + 1) * half].astype(f32)
        for k in range(3):
            total = total + rw[part, k].astype(f32)
        return total

    grad_rows(0, second_g, hh)
    w_grads(1, 0)
    grad_rows(1, cot_g, act)
    w_grads(1, 1)
    second_grad = share_total(0)
    cotangent = cot_ref[...].astype(f32)
    middle_grad = cotangent + normalize_back(second_grad, norm2[...], inv_second, gains_ref[1:2])
    mgrad[...] = middle_grad
    middle_half = middle_grad.astype(bf16)
    midb[...] = middle_half
    c2a = slot(2 * nt)
    slabs = matmul(middle_half, fo[...]).astype(bf16)
    for j in range(nt):
        slab = slabs[:, j * E : (j + 1) * E]

        @pl.when(t == j)
        def _():
            cg[blk(t), :] = slab

        @pl.when(t != j)
        def _():
            cgs[j] = slab
            remote(
                cgs.at[j], cg.at[blk(t)], ss.at[c2a + j], rs.at[c2a + t], {"tensor": j}
            ).start()

    po[...] = contract_rows(midb[...], call[...]).astype(bf16)
    og = [link(po.at[core_rows(k, 1 - core)], ao.at[k], partner) for k in range(4)]
    w_grads(0, 0, 2)
    small[1:2, :] = jnp.sum(second_grad * norm2[...], axis=0, keepdims=True)
    small[3:4, :] = jnp.sum(second_grad, axis=0, keepdims=True)
    small[4:5, :] = jnp.sum(middle_grad, axis=0, keepdims=True)
    small[5:6, :] = jnp.sum(cotangent, axis=0, keepdims=True)
    for s in (3, 1, 2, 0):
        share(1, s, contract_cols(act[member(s), :], fw[1]))
    share_near(1)

    for k in range(1, nt):
        src = other(k)
        remote(cg.at[blk(src)], cg.at[blk(src)], ss.at[c2a], rs.at[c2a + src], far).wait_recv()

    r2a = slot(2 * nt)
    og2 = {}
    for b in reversed(range(nt)):
        low = max(0, b - reach)
        width = (b + 1 - low) * T
        here, window = slice(b * T, (b + 1) * T), slice(low * T, (b + 1) * T)
        query_parts = []
        for h in range(heads):
            cols = slice(h * HEAD, (h + 1) * HEAD)
            prob = probs[h, b, :, :width]
            grad = cg[here, cols]
            prob_grad = contract_cols(grad, vs[window, cols])
            row_dot = jnp.sum(
                grad.astype(f32) * ctx[here, cols].astype(f32), axis=-1, keepdims=True
            )
            score_grad = (prob * (prob_grad - row_dot) * inv_root).astype(bf16)
            query_grad = matmul(score_grad, ks[window, cols])
            query_parts.append(query_grad)
            key_part = contract_rows(score_grad, qs[here, cols])
            value_part = contract_rows(prob.astype(bf16), grad)
            for j in range(low, b + 1):
                at = slice((j - low) * T, (j - low + 1) * T)
                to = slice(j * T, (j + 1) * T)
                if b == min(j + reach, nt - 1):
                    kacc[h, to, :] = key_part[at]
                    vacc[h, to, :] = value_part[at]
                else:
                    kacc[h, to, :] += key_part[at]
                    vacc[h, to, :] += value_part[at]
        query_rows = jnp.concatenate(query_parts, axis=1)
        value_rows = jnp.concatenate([vacc[h, here, :] for h in range(heads)], axis=1)
        key_rows = jnp.concatenate([kacc[h, here, :] for h in range(heads)], axis=1)
        block = jnp.concatenate([query_rows, key_rows, value_rows], axis=1).astype(bf16)
        ph[here, :] = block
        small[9:10, :E] += jnp.sum(query_rows, axis=0, keepdims=True)
        small[10:11, :E] += jnp.sum(value_rows, axis=0, keepdims=True)
        first_share = contract_cols(block, fq[...])

        @pl.when(t == b)
        def _():
            fown[...] = first_share

        @pl.when(t != b)
        def _():
            fsend[b] = first_share.astype(bf16)
            remote(
                fsend.at[b], frecv.at[t], ss.at[r2a + b], rs.at[r2a + t], {"tensor": b}
            ).start()

        if b == nt - 1:
            for k in (1, 2, 3, 0):
                og[k].wait_recv()
                total = po[core_rows(k, core), :].astype(f32) + ao[k].astype(f32)
                if k:
                    bo[k - 1] = total.astype(bf16)
                    og2[k] = link(bo.at[k - 1], ro.at[k - 1], along[k])
                else:
                    ozw[...] = total
        if b == nt - 2:
            h_far.wait_recv()
            small[8:9, mine] = hsum[0:1, :half] + hrecv[0:1]
            wz[...] = w_sum(1, (0, 1)).astype(bf16)
            wz_in = link(wz, wzr, far)

    def chunk(c, carry):
        pq[blk(c, step), :] = contract_rows(first_ref[:, blk(c, step)], ph[...]).astype(bf16)
        return carry

    lax.fori_loop(0, D // step, chunk, 0)
    qg = [link(pq.at[core_rows(k, 1 - core)], aq.at[k], partner) for k in (0, 1, 2, 3)]
    qg2 = {}
    for k in (1, 2, 3, 0):
        qg[k].wait_recv()
        total = pq[core_rows(k, core), :].astype(f32) + aq[k].astype(f32)
        if k:
            bq[k - 1] = total.astype(bf16)
            qg2[k] = link(bq.at[k - 1], rq.at[k - 1], along[k])
        else:
            oq[...] = total

    out_total = ozw[...]
    for k in (1, 2, 3):
        og2[k].wait_recv()
        out_total = out_total + ro[k - 1].astype(f32)
    for j in range(nt):
        oz[j] = out_total[:, j * E : (j + 1) * E]
        ozs[j] = oz[j].astype(bf16)
    z2a = slot(2 * nt)
    for k in range(1, nt):
        copy = remote(
            ozs.at[other(k)], ozt.at[t], ss.at[z2a + k], rs.at[z2a + t], {"tensor": other(k)}
        )
        copy.start()
        sent.append(copy)

    bo_ref[...] = (mid[...] + share_total(1) + biases_ref[3:4]).astype(bf16)
    own_sum = w_sum(0, (0,))
    wz_in.wait_recv()
    wsum[...] = own_sum + wzr[...].astype(f32)
    wx_in = link(wsum.at[:, blk(1 - core, rows), :], wx, partner)

    first_grad = fown[...]
    for k in range(1, nt):
        src = other(k)
        remote(frecv.at[src], frecv.at[src], ss.at[r2a], rs.at[r2a + src], far).wait_recv()
        first_grad = first_grad + frecv[src].astype(f32)
    ig_ref[...] = mgrad[...] + normalize_back(first_grad, norm1[...], inv_first, gains_ref[0:1])
    small[0:1, :] = jnp.sum(first_grad * norm1[...], axis=0, keepdims=True)
    small[2:3, :] = jnp.sum(first_grad, axis=0, keepdims=True)
    zsmall[t] = small[0:8, :]
    zin = [link(zsmall.at[t], zsmall.at[t], {"tensor": other(k)}) for k in range(1, nt)]

    out_total = oz[t]
    for k in range(1, nt):
        src = other(k)
        remote(ozt.at[src], ozt.at[src], ss.at[z2a], rs.at[z2a + src], far).wait_recv()
        out_total = out_total + ozt[src].astype(f32)
    go_ref[...] = jnp.transpose(out_total)

    for copy in zin:
        copy.wait_recv()
    summed = zsmall[0]
    for k in range(1, nt):
        summed = summed + zsmall[k]
    psmall[core] = jnp.concatenate([summed, small[8:16, :]], axis=0)
    pin = link(psmall.at[core], psmall.at[core], partner)
    total = oq[...]
    for k in (1, 2, 3):
        qg2[k].wait_recv()
        total = total + rq[k - 1].astype(f32)
    for c in range(3):
        gq_ref[c] = total[:, c * E : (c + 1) * E]
    pin.wait_recv()
    csmall[chip] = psmall[0] + psmall[1]
    cin = [link(csmall.at[chip], csmall.at[chip], along[k]) for k in (1, 2, 3)]
    wx_in.wait_recv()
    for w, ref in ((0, gi_ref), (1, gb_ref)):
        ref[:, mine] = wsum[w, blk(core, rows), :]
        ref[:, theirs] = wx[w]
    for copy in cin:
        copy.wait_recv()
    total = csmall[0]
    for c in range(1, nc):
        total = total + csmall[c]
    gqv_ref[...] = total[9:11, :E]
    ginb_ref[...] = total[8:9, :F]
    ggain_ref[...] = total[0:2]
    gbias_ref[...] = total[2:6]
    gather_drain(0, first_ref)
    for base, piece in ((a2a, ctx.at[pl.ds(0, T)]), (c2a, cgs.at[0]), (r2a, fsend.at[0])):
        for b in range(nt):

            @pl.when(t != b)
            def _():
                remote(piece, piece, ss.at[base + b], rs.at[base + b], far).wait_send()

    for copy in sent:
        copy.wait_send()


def hand_over(*refs):
    n = (len(refs) - 2) // 3
    held, sems = refs[2 * n : 3 * n], refs[3 * n :]
    loads = [pltpu.make_async_copy(refs[i], held[i], sems[0].at[i]) for i in range(n)]
    stores = [pltpu.make_async_copy(held[i], refs[n + i], sems[1].at[i]) for i in range(n)]
    for copy in loads:
        copy.start()
    for load, store in zip(loads, stores):
        load.wait()
        store.start()
    for copy in stores:
        copy.wait()


def kernel_shards(
    nt,
    nd,
    block_input,
    segment_ids,
    w_qkv,
    w_out,
    w_in,
    w_back,
    qv_bias,
    in_bias,
    norm_gains,
    norm_biases,
    out_cotangent,
):
    bf16, f32 = jnp.bfloat16, jnp.float32
    T, D = block_input.shape[1:]
    E, F = w_qkv.shape[2], w_in.shape[1]
    rows = D // nd
    seq = nt * T
    heads = E // HEAD
    nc = nd // 2
    half = F // 2
    reach = (seq // 2 - 1 + T - 1) // T
    window = min(nt, reach + 1) * T
    group = 4 * T
    vm = pltpu.VMEM
    scratch = [
        vm((D, 3 * E), bf16),
        vm((D, nt * E), bf16),
        vm((nt, rows, E), bf16),
        vm((2, D, F), bf16),
        vm((seq, D), bf16),
        vm((group, D), bf16),
        vm((group, D), bf16),
        vm((T, D), bf16),
        vm((nt, 8, T), jnp.int32),
        vm((seq, E), bf16),
        vm((seq, E), bf16),
        vm((seq, E), bf16),
        vm((seq, E), bf16),
        vm((nt, T, E), bf16),
        vm((T, nt * E), bf16),
        vm((nt, T, E), bf16),
        vm((seq, E), bf16),
        vm((heads, nt, T, window), f32),
        vm((group, F), f32),
        vm((group, F), bf16),
        vm((group, F), bf16),
        vm((seq, 3 * E), bf16),
        vm((heads, seq, HEAD), f32),
        vm((heads, seq, HEAD), f32),
        vm((nt, T, D), bf16),
        vm((nt, T, D), bf16),
        vm((2, 2, T, D), f32),
        vm((2, 3, T, D), bf16),
        vm((2, 3, T, D), bf16),
        vm((T, D), f32),
        vm((T, D), f32),
        vm((T, D), f32),
        vm((T, D), f32),
        vm((T, D), f32),
        vm((2, D, F), bf16),
        vm((2, 3, 2, 2 * rows, half), bf16),
        vm((2, 2 * rows, half), bf16),
        vm((2, 2 * rows, half), bf16),
        vm((2, 2 * rows, half), f32),
        vm((2, rows, half), f32),
        vm((D, 3 * E), bf16),
        vm((nc, rows, 3 * E), bf16),
        vm((nc - 1, rows, 3 * E), bf16),
        vm((nc - 1, rows, 3 * E), bf16),
        vm((rows, 3 * E), f32),
        vm((D, nt * E), bf16),
        vm((nc, rows, nt * E), bf16),
        vm((nc - 1, rows, nt * E), bf16),
        vm((nc - 1, rows, nt * E), bf16),
        vm((rows, nt * E), f32),
        vm((nt, rows, E), f32),
        vm((nt, rows, E), bf16),
        vm((nt, rows, E), bf16),
        vm((2, 8, half), f32),
        vm((8, F), f32),
        vm((8, half), f32),
        vm((16, D), f32),
        vm((nt, 8, D), f32),
        vm((2, 16, D), f32),
        vm((nc, 16, D), f32),
        pltpu.SemaphoreType.DMA((1, 2 * nt)),
        pltpu.SemaphoreType.DMA((1, 2 * nt)),
        pltpu.SemaphoreType.DMA((128,)),
        pltpu.SemaphoreType.DMA((128,)),
    ]
    spec = pl.BlockSpec(memory_space=pltpu.VMEM)
    outs = pl.pallas_call(
        functools.partial(layer_kernel, nt, nd),
        out_shape=[
            jax.ShapeDtypeStruct((T, D), bf16),
            jax.ShapeDtypeStruct((T, D), f32),
            jax.ShapeDtypeStruct((3, rows, E), f32),
            jax.ShapeDtypeStruct((E, rows), f32),
            jax.ShapeDtypeStruct((rows, F), f32),
            jax.ShapeDtypeStruct((rows, F), f32),
            jax.ShapeDtypeStruct((2, E), f32),
            jax.ShapeDtypeStruct((1, F), f32),
            jax.ShapeDtypeStruct((2, D), f32),
            jax.ShapeDtypeStruct((4, D), f32),
        ],
        in_specs=[spec] * 11,
        out_specs=[spec] * 10,
        scratch_shapes=scratch,
        compiler_params=pltpu.CompilerParams(
            collective_id=0, has_side_effects=True, vmem_limit_bytes=60 * 1024 * 1024
        ),
        name="layer",
    )(
        block_input[0],
        segment_ids,
        w_qkv,
        w_out,
        w_in,
        w_back.T,
        out_cotangent[0],
        qv_bias,
        in_bias[None],
        norm_gains,
        norm_biases,
    )
    outs = pl.pallas_call(
        hand_over,
        out_shape=[jax.ShapeDtypeStruct(a.shape, a.dtype) for a in outs],
        in_specs=[pl.BlockSpec(memory_space=pl.ANY)] * 10,
        out_specs=[pl.BlockSpec(memory_space=pl.ANY)] * 10,
        scratch_shapes=[vm(a.shape, a.dtype) for a in outs]
        + [pltpu.SemaphoreType.DMA((10,))] * 2,
        name="hand_over",
    )(*outs)
    block_out, input_grad, gq, go, gi, gb, gqv, ginb, ggain, gbias = outs
    return (block_out[None], input_grad[None], gq, go, gi, gb.T, gqv, ginb[0], ggain, gbias)


def solution(mesh):
    in_specs = (
        P("dp", "tensor", None),
        P("dp", "tensor"),
        P(None, "dp", "tensor"),
        P("tensor", "dp"),
        P("dp", "tensor"),
        P("tensor", "dp"),
        P(None, "tensor"),
        P("tensor"),
        P(),
        P(),
        P("dp", "tensor", None),
    )
    out_specs = (
        P("dp", "tensor", None),
        P("dp", "tensor", None),
        P(None, "dp", "tensor"),
        P("tensor", "dp"),
        P("dp", "tensor"),
        P("tensor", "dp"),
        P(None, "tensor"),
        P("tensor"),
        P(),
        P(),
    )
    nt, nd = mesh.shape["tensor"], mesh.shape["dp"]

    def body(*args):
        block_input, w_qkv, w_in = args[0], args[2], args[4]
        tokens, features = block_input.shape[1:]
        fits = (
            nt == 4
            and nd == 2 * nt
            and w_in.shape[0] % 16 == 0
            and w_in.shape[1] % 256 == 0
            and tokens % 128 == 0
            and features % 128 == 0
            and w_in.shape[1] <= features
            and w_qkv.shape[2] % HEAD == 0
        )
        if fits:
            return kernel_shards(nt, nd, *args)
        return shards(*args)

    return jax.shard_map(body, mesh=mesh, in_specs=in_specs, out_specs=out_specs, check_vma=False)
```

```python
import functools
import math

import jax
import jax.numpy as jnp
from jax import lax
from jax.experimental import pallas as pl
from jax.experimental.pallas import tpu as pltpu
from jax.sharding import PartitionSpec as P

HEAD = 64


EPS = 1e-05
GELU_C = math.sqrt(2.0 / math.pi)
GELU_A = 0.044715


def normalize(residual, gain_row, offset_row):
    centered = residual - jnp.mean(residual, axis=-1, keepdims=True)
    inv_std = lax.rsqrt(jnp.mean(centered * centered, axis=-1, keepdims=True) + EPS)
    normed = centered * inv_std
    return (normed * gain_row + offset_row, normed, inv_std)


def normalize_back(upstream, normed, inv_std, gain_row):
    scaled = upstream * gain_row
    return inv_std * (
        scaled
        - jnp.mean(scaled, axis=-1, keepdims=True)
        - normed * jnp.mean(scaled * normed, axis=-1, keepdims=True)
    )


def gelu_pair(inputs):
    inner_arg = GELU_C * (inputs + GELU_A * inputs * inputs * inputs)
    tangent_h = jnp.tanh(inner_arg)
    value_out = 0.5 * inputs * (1.0 + tangent_h)
    slope_out = 0.5 * (1.0 + tangent_h) + 0.5 * inputs * (1.0 - tangent_h * tangent_h) * GELU_C * (
        1.0 + 3.0 * GELU_A * inputs * inputs
    )
    return (value_out, slope_out)


def contract_rows(left, right):
    return lax.dot_general(
        left, right, (((0,), (0,)), ((), ())), preferred_element_type=jnp.float32
    )


def contract_cols(left, right):
    return lax.dot_general(
        left, right, (((1,), (1,)), ((), ())), preferred_element_type=jnp.float32
    )


def masked_scores(query_block, key_rows, segment, key_end, num_heads):
    block_rows = query_block.shape[0]
    width = query_block.shape[1] // num_heads
    query_heads = query_block.reshape(block_rows, num_heads, width)
    key_heads = key_rows.reshape(key_end, num_heads, width)
    raw_scores = jnp.einsum(
        "qhd,khd->hqk", query_heads, key_heads, preferred_element_type=jnp.float32
    ) * (1.0 / math.sqrt(width))
    query_pos = jnp.arange(block_rows, dtype=jnp.int32)
    key_pos = jnp.arange(key_end, dtype=jnp.int32)
    allowed = (key_pos[None, :] <= query_pos[:, None]) & (segment[None, :] == segment[:, None])
    return jnp.where(allowed[None], raw_scores, -jnp.inf)


def attend_forward(queries, key_rows, values, segment, num_heads):
    total_rows = queries.shape[0]
    block_rows = min(512, total_rows)
    width = queries.shape[1] // num_heads
    scores = masked_scores(queries, key_rows, segment, block_rows, num_heads)
    row_max = jnp.max(scores, axis=-1, keepdims=True)
    log_total = row_max + jnp.log(jnp.sum(jnp.exp(scores - row_max), axis=-1, keepdims=True))
    weights = jnp.exp(scores - log_total).astype(jnp.bfloat16)
    value_heads = values.reshape(block_rows, num_heads, width)
    context = jnp.einsum("hqk,khd->qhd", weights, value_heads, preferred_element_type=jnp.float32)
    contexts = context.reshape(block_rows, num_heads * width).astype(jnp.bfloat16)
    return (contexts, log_total)


def attend_backward(
    queries, key_rows, values, segment, context, log_total, context_grad, num_heads
):
    total_rows = queries.shape[0]
    block_rows = min(512, total_rows)
    width = queries.shape[1] // num_heads
    inv_root = 1.0 / math.sqrt(width)
    key_grad = jnp.zeros((total_rows, num_heads, width), jnp.float32)
    value_grad = jnp.zeros((total_rows, num_heads, width), jnp.float32)
    scores = masked_scores(queries, key_rows, segment, block_rows, num_heads)
    probs = jnp.exp(scores - log_total)
    probs_half = probs.astype(jnp.bfloat16)
    grad_heads = context_grad.reshape(block_rows, num_heads, width)
    context_heads = context.reshape(block_rows, num_heads, width)
    value_heads = values.reshape(block_rows, num_heads, width)
    key_heads = key_rows.reshape(block_rows, num_heads, width)
    query_heads = queries.reshape(block_rows, num_heads, width)
    prob_grad = jnp.einsum(
        "qhd,khd->hqk", grad_heads, value_heads, preferred_element_type=jnp.float32
    )
    row_dot = jnp.transpose(
        jnp.sum(grad_heads.astype(jnp.float32) * context_heads.astype(jnp.float32), axis=-1)
    )[:, :, None]
    score_grad = (probs * (prob_grad - row_dot) * inv_root).astype(jnp.bfloat16)
    query_grads = jnp.einsum(
        "hqk,khd->qhd", score_grad, key_heads, preferred_element_type=jnp.float32
    ).reshape(block_rows, num_heads * width)
    key_grad = key_grad.at[:block_rows].add(
        jnp.einsum("hqk,qhd->khd", score_grad, query_heads, preferred_element_type=jnp.float32)
    )
    value_grad = value_grad.at[:block_rows].add(
        jnp.einsum("hqk,qhd->khd", probs_half, grad_heads, preferred_element_type=jnp.float32)
    )
    return (
        query_grads,
        key_grad.reshape(total_rows, num_heads * width),
        value_grad.reshape(total_rows, num_heads * width),
    )


def half_scatter(share):
    return lax.psum_scatter(
        share.astype(jnp.bfloat16), "tensor", scatter_dimension=0, tiled=True
    ).astype(jnp.float32)


def shards(
    block_input,
    segment_ids,
    w_qkv,
    w_out,
    w_in,
    w_back,
    qv_bias,
    in_bias,
    norm_gains,
    norm_biases,
    out_cotangent,
):
    bf16 = jnp.bfloat16
    residual = block_input[0].astype(jnp.float32)
    head_cols = w_qkv.shape[2]
    hidden_cols = w_in.shape[1]
    local_heads = head_cols // HEAD
    cuts = [head_cols, 2 * head_cols, 3 * head_cols, 4 * head_cols, 4 * head_cols + hidden_cols]
    packed = jnp.concatenate([w_qkv[0], w_qkv[1], w_qkv[2], w_out.T, w_in, w_back.T], axis=1)
    full = lax.all_gather(packed, "dp", axis=0, tiled=True)
    qkv_full = full[:, : cuts[2]]
    out_full = full[:, cuts[2] : cuts[3]]
    in_full = full[:, cuts[3] : cuts[4]]
    back_full = full[:, cuts[4] :]
    first_out, normed_first, inv_first = normalize(residual, norm_gains[0], norm_biases[0])
    first_half, segment, cotangent_full = (
        lax.all_gather(first_out.astype(bf16), "tensor", axis=0, tiled=True),
        lax.all_gather(segment_ids[0], "tensor", axis=0, tiled=True),
        lax.all_gather(out_cotangent[0], "tensor", axis=0, tiled=True),
    )
    projected = jnp.dot(first_half, qkv_full, preferred_element_type=jnp.float32)
    queries = (projected[:, : cuts[0]] + qv_bias[0]).astype(bf16)
    key_rows = projected[:, cuts[0] : cuts[1]].astype(bf16)
    values = (projected[:, cuts[1] :] + qv_bias[1]).astype(bf16)
    context, log_total = attend_forward(queries, key_rows, values, segment, local_heads)
    attn_share = half_scatter(contract_cols(context, out_full))
    middle = residual + attn_share + norm_biases[2]
    second_out, normed_second, inv_second = normalize(middle, norm_gains[1], norm_biases[1])
    second_half = lax.all_gather(second_out.astype(bf16), "tensor", axis=0, tiled=True)
    hidden_pre = jnp.dot(second_half, in_full, preferred_element_type=jnp.float32) + in_bias
    gelu_value, gelu_slope = gelu_pair(hidden_pre)
    activation = gelu_value.astype(bf16)
    mlp_share = half_scatter(contract_cols(activation, back_full))
    block_out = (middle + mlp_share + norm_biases[3]).astype(bf16)
    cotangent = out_cotangent[0].astype(jnp.float32)
    grad_back_part = contract_rows(cotangent_full, activation)
    hidden_grad = jnp.dot(cotangent_full, back_full, preferred_element_type=jnp.float32) * gelu_slope
    hidden_half = hidden_grad.astype(bf16)
    grad_in_part = contract_rows(second_half, hidden_half)
    second_grad = half_scatter(contract_cols(hidden_half, in_full))
    middle_grad = cotangent + normalize_back(second_grad, normed_second, inv_second, norm_gains[1])
    middle_full = lax.all_gather(middle_grad.astype(bf16), "tensor", axis=0, tiled=True)
    grad_out_part = contract_rows(middle_full, context)
    context_grad = jnp.dot(middle_full, out_full, preferred_element_type=jnp.float32).astype(bf16)
    query_grad, key_grad, value_grad = attend_backward(
        queries, key_rows, values, segment, context, log_total, context_grad, local_heads
    )
    proj_half = jnp.concatenate([query_grad, key_grad, value_grad], axis=1).astype(bf16)
    grad_qkv_part = contract_rows(first_half, proj_half)
    first_grad = half_scatter(contract_cols(proj_half, qkv_full))
    input_grad = middle_grad + normalize_back(first_grad, normed_first, inv_first, norm_gains[0])
    parts = jnp.concatenate(
        [grad_qkv_part, grad_out_part, grad_in_part, grad_back_part], axis=1
    ).astype(bf16)
    grads = lax.psum_scatter(parts, "dp", scatter_dimension=0, tiled=True).astype(jnp.float32)
    grad_qkv = jnp.stack([grads[:, : cuts[0]], grads[:, cuts[0] : cuts[1]], grads[:, cuts[1] : cuts[2]]])
    grad_out = grads[:, cuts[2] : cuts[3]].T
    grad_in = grads[:, cuts[3] : cuts[4]]
    grad_back = grads[:, cuts[4] :].T
    own = jnp.concatenate(
        [jnp.sum(query_grad, axis=0), jnp.sum(value_grad, axis=0), jnp.sum(hidden_grad, axis=0)]
    )
    tensors = lax.axis_size("tensor")
    rank = lax.axis_index("tensor")
    spread = jnp.where(jnp.arange(tensors)[:, None] == rank, own[None], 0.0)
    norm_terms = jnp.stack(
        [
            jnp.sum(first_grad * normed_first, axis=0),
            jnp.sum(second_grad * normed_second, axis=0),
            jnp.sum(first_grad, axis=0),
            jnp.sum(second_grad, axis=0),
            jnp.sum(middle_grad, axis=0),
            jnp.sum(cotangent, axis=0),
        ]
    )
    total = lax.psum(
        jnp.concatenate([spread.reshape(-1), norm_terms.reshape(-1)]), ("dp", "tensor")
    )
    width = own.shape[0]
    own_total = lax.dynamic_slice(total, (rank * width,), (width,))
    norm_total = total[tensors * width :].reshape(norm_terms.shape)
    return (
        block_out[None],
        input_grad[None],
        grad_qkv,
        grad_out,
        grad_in,
        grad_back,
        own_total[: 2 * head_cols].reshape(2, head_cols),
        own_total[2 * head_cols :],
        norm_total[:2],
        norm_total[2:],
    )


def matmul(left, right):
    return jnp.dot(left, right, preferred_element_type=jnp.float32)


def layer_kernel(
    nt,
    nd,
    x_ref,
    seg_ref,
    wq_ref,
    wo_ref,
    wi_ref,
    wb_ref,
    cot_ref,
    qvb_ref,
    inb_ref,
    gains_ref,
    biases_ref,
    bo_ref,
    ig_ref,
    gq_ref,
    go_ref,
    gi_ref,
    gb_ref,
    gqv_ref,
    ginb_ref,
    ggain_ref,
    gbias_ref,
    fq,
    fo,
    own_out,
    fw,
    first_ref,
    second_g,
    cot_g,
    midb,
    segs,
    qs,
    ks,
    vs,
    ctx,
    ctx_all,
    call,
    cgs,
    cg,
    probs,
    hb,
    act,
    hh,
    ph,
    kacc,
    vacc,
    fsend,
    frecv,
    shares,
    share_out,
    share_in,
    mid,
    norm1,
    norm2,
    mgrad,
    fown,
    fpass,
    fhold,
    pw,
    rw,
    wz,
    wzr,
    wsum,
    wx,
    pq,
    aq,
    bq,
    rq,
    oq,
    po,
    ao,
    bo,
    ro,
    ozw,
    oz,
    ozs,
    ozt,
    inbs,
    hsum,
    hrecv,
    small,
    zsmall,
    psmall,
    csmall,
    gs,
    gr,
    ss,
    rs,
):
    bf16 = jnp.bfloat16
    f32 = jnp.float32
    nc = nd // 2
    t = lax.axis_index("tensor")
    d = lax.axis_index("dp")
    core = lax.rem(d, 2)
    chip = d // 2
    T, D = x_ref.shape
    rows = wi_ref.shape[0]
    E = ctx.shape[1]
    F = wi_ref.shape[1]
    half = F // 2
    heads = E // HEAD
    seq = nt * T
    cy, cx = chip // 2, lax.rem(chip, 2)
    chips = (chip, cy * 2 + 1 - cx, (1 - cy) * 2 + cx, (1 - cy) * 2 + 1 - cx)
    partner = {"dp": chip * 2 + 1 - core}
    along = [{"dp": c * 2 + core} for c in chips]
    near = {"tensor": t + 1 - 2 * lax.rem(t, 2)}
    far = {"tensor": lax.rem(t + 2, nt)}

    def remote(src, dst, ssem, rsem, where):
        return pltpu.make_async_remote_copy(
            src_ref=src,
            dst_ref=dst,
            send_sem=ssem,
            recv_sem=rsem,
            device_id=where,
            device_id_type=pl.DeviceIdType.MESH,
        )

    used = []
    sent = []

    def slot(count=1):
        used.extend([0] * count)
        return len(used) - count

    def link(src, dst, where):
        i = slot()
        copy = remote(src, dst, ss.at[i], rs.at[i], where)
        copy.start()
        sent.append(copy)
        return copy

    def link_all(piece, places):
        return [link(piece, piece, where) for where in places]

    def blk(index, size=T):
        return pl.ds(pl.multiple_of(index * size, size), size)

    def chip_rows(k):
        return blk(chips[k], 2 * rows)

    def core_rows(k, c):
        return blk(chips[k] * 2 + c, rows)

    def other(k):
        return lax.rem(t + k, nt)

    def line_copy(kind, place, ref, b, to):
        piece = ref.at[blk(b)]
        return remote(piece, piece, gs.at[kind, place], gr.at[kind, b], {"tensor": to})

    def line_own(kind, ref, act_on):
        for place, to in ((0, t + 1), (2 * nt - 1, t - 1)):

            @pl.when((to >= 0) & (to < nt))
            def _():
                act_on(line_copy(kind, place, ref, t, to))

    def line_place(s):
        sign = 2 * (s % 2) - 1
        return t + sign * ((s + 1) // 2), t - sign

    def gather_send(kind, ref):
        line_own(kind, ref, lambda copy: copy.start())

    def gather_step(kind, ref, s):
        b, to = line_place(s)

        @pl.when((b >= 0) & (b < nt))
        def _():
            remote(
                ref.at[blk(b)], ref.at[blk(b)], gs.at[kind, 0], gr.at[kind, b], {"tensor": b}
            ).wait_recv()

            @pl.when((to >= 0) & (to < nt))
            def _():
                line_copy(kind, s, ref, b, to).start()

    def gather_drain(kind, ref):
        line_own(kind, ref, lambda copy: copy.wait_send())

        for s in range(1, 2 * nt - 1):
            b, to = line_place(s)

            @pl.when((b >= 0) & (b < nt) & (to >= 0) & (to < nt))
            def _():
                line_copy(kind, s, ref, b, to).wait_send()

    barrier = pltpu.get_barrier_semaphore()
    for where in [{"tensor": other(k)} for k in range(1, nt)] + along[1:] + [partner]:
        pl.semaphore_signal(barrier, inc=1, device_id=where, device_id_type=pl.DeviceIdType.MESH)
    residual = x_ref[...].astype(f32)
    first_out, normed_first, inv_first = normalize(residual, gains_ref[0:1], biases_ref[0:1])
    norm1[...] = normed_first
    first_ref[blk(t), :] = first_out.astype(bf16)
    fq[blk(d, rows), :] = jnp.concatenate([wq_ref[0], wq_ref[1], wq_ref[2]], axis=1)
    own_out[t] = jnp.transpose(wo_ref[...].astype(f32)).astype(bf16)
    mine, theirs = blk(core, half), blk(1 - core, half)
    fw[0, blk(d, rows), :half] = wi_ref[:, mine]
    fw[1, blk(d, rows), :half] = wb_ref[:, mine]
    segs[t] = jnp.broadcast_to(seg_ref[...], segs.shape[1:])
    inbs[0] = jnp.broadcast_to(inb_ref[:, mine], inbs.shape[1:])
    pl.semaphore_wait(barrier, nt - 1 + nc - 1 + 1)

    gather_send(0, first_ref)
    own_rows = blk(d, rows)
    lines = [{"tensor": other(k)} for k in range(1, nt)]
    q_piece = fq.at[own_rows]
    q_in = link_all(q_piece, along[1:])
    w_pair = [
        link(ref.at[:, theirs], fw.at[w, own_rows, pl.ds(0, half)], partner)
        for w, ref in ((0, wi_ref), (1, wb_ref))
    ]
    q_pair = link_all(q_piece, [partner])
    seg_in = link_all(segs.at[t], lines)
    cot_pair = link(cot_ref, cot_g.at[pl.ds(T, T)], partner)
    cot_g[0:T] = cot_ref[...]

    w_in = {}

    def w_send(part, w, n=1):
        piece = fw.at[pl.ds(w, n), chip_rows(0), pl.ds(part * half, half)]
        w_in[part, w, 1], w_in[part, w, 2] = link_all(piece, along[1:3])

    def w_forward(part, w, n=1):
        cols = pl.ds(part * half, half)
        w_in[part, w, 1].wait_recv()
        piece = fw.at[pl.ds(w, n), core_rows(1, 0), cols]
        w_in[part, w, 3] = link(piece, piece, along[2])
        w_in[part, w, 2].wait_recv()
        piece = fw.at[pl.ds(w, n), core_rows(2, 1), cols]
        w_in[part, w, 4] = link(piece, piece, along[1])

    def w_wait(part, w):
        w_in[part, w, 3].wait_recv()
        w_in[part, w, 4].wait_recv()

    for copy in w_pair:
        copy.wait_recv()
    w_send(0, 0, 2)
    w_far = [
        link(
            fw.at[w, chip_rows(0), pl.ds(0, half)], fw.at[w, chip_rows(0), pl.ds(half, half)], far
        )
        for w in (1, 0)
    ]
    inb_far = link(inbs.at[0], inbs.at[1], far)
    gather_step(0, first_ref, 1)
    gather_step(0, first_ref, 2)
    o_line = [link(own_out.at[t], own_out.at[t], where) for where in lines]
    for k in (1, 2, 3):
        q_in[k - 1].wait_recv()
        q_pair += link_all(fq.at[core_rows(k, core)], [partner])
    gather_step(0, first_ref, 3)
    gather_step(0, first_ref, 4)
    for copy in o_line:
        copy.wait_recv()
    fo[own_rows, :] = jnp.concatenate([own_out[j] for j in range(nt)], axis=1)
    o_pair = link_all(fo.at[own_rows], [partner])
    o_in = link_all(fo.at[own_rows], along[1:])
    w_forward(0, 0, 2)
    for s in range(5, 2 * nt - 1):
        gather_step(0, first_ref, s)
    cot_near = link(cot_ref, cot_g.at[pl.ds(2 * T, T)], near)
    for copy in q_pair:
        copy.wait_recv()

    inv_root = 1.0 / math.sqrt(HEAD)
    projected = matmul(first_ref[...], fq[...])
    qs[...] = (projected[:, :E] + qvb_ref[0:1]).astype(bf16)
    ks[...] = projected[:, E : 2 * E].astype(bf16)
    vs[...] = (projected[:, 2 * E :] + qvb_ref[1:2]).astype(bf16)
    for copy in seg_in:
        copy.wait_recv()

    reach = (seq // 2 - 1 + T - 1) // T
    a2a = slot(2 * nt)
    for b in range(nt):
        low = max(0, b - reach)
        width = (b + 1 - low) * T
        key_seg = jnp.concatenate([segs[j][0:1].astype(f32) for j in range(low, b + 1)], axis=1)
        query_seg = jnp.transpose(jnp.broadcast_to(segs[b][0:1].astype(f32), (T, T)))[:, 0:1]
        query_pos = lax.broadcasted_iota(jnp.int32, (T, width), 0) + b * T
        key_pos = lax.broadcasted_iota(jnp.int32, (T, width), 1) + low * T
        allowed = (key_pos <= query_pos) & (query_seg == key_seg)
        for h in range(heads):
            cols = slice(h * HEAD, (h + 1) * HEAD)
            scores = (
                contract_cols(qs[b * T : (b + 1) * T, cols], ks[low * T : (b + 1) * T, cols])
                * inv_root
            )
            scores = jnp.where(allowed, scores, -jnp.inf)
            row_max = jnp.max(scores, axis=-1, keepdims=True)
            powers = jnp.exp(scores - row_max)
            prob = powers * (1.0 / jnp.sum(powers, axis=-1, keepdims=True))
            probs[h, b, :, :width] = prob
            ctx[b * T : (b + 1) * T, cols] = matmul(
                prob.astype(bf16), vs[low * T : (b + 1) * T, cols]
            ).astype(bf16)

        @pl.when(t == b)
        def _():
            ctx_all[t] = ctx[b * T : (b + 1) * T, :]

        @pl.when(t != b)
        def _():
            remote(
                ctx.at[pl.ds(b * T, T)], ctx_all.at[t], ss.at[a2a + b], rs.at[a2a + t], {"tensor": b}
            ).start()

    for k in (1, 2, 3):
        o_in[k - 1].wait_recv()
        o_pair += link_all(fo.at[core_rows(k, core)], [partner])
    for n, w in enumerate((1, 0)):
        w_far[n].wait_recv()
        w_send(1, w)
    for k in range(1, nt):
        src = other(k)
        remote(ctx_all.at[src], ctx_all.at[src], ss.at[a2a], rs.at[a2a + src], far).wait_recv()
    call[...] = jnp.concatenate([ctx_all[j] for j in range(nt)], axis=1)
    for copy in o_pair:
        copy.wait_recv()
    middle = residual + contract_cols(call[...], fo[...]) + biases_ref[2:3]
    mid[...] = middle
    second_out, normed_second, inv_second = normalize(middle, gains_ref[1:2], biases_ref[1:2])
    norm2[...] = normed_second
    second_g[0:T] = second_out.astype(bf16)
    second_piece = second_g.at[pl.ds(0, T)]
    s_near = link(second_piece, second_g.at[pl.ds(2 * T, T)], near)
    s_pair = link(second_piece, second_g.at[pl.ds(T, T)], partner)
    w_forward(1, 1)
    w_wait(0, 0)
    inb_far.wait_recv()
    cot_near.wait_recv()
    cot_pair2 = link(cot_g.at[pl.ds(2 * T, T)], cot_g.at[pl.ds(3 * T, T)], partner)
    cot_pair.wait_recv()

    def member(s):
        return slice(s * T, (s + 1) * T)

    def back(s):
        hb[member(s), :] = matmul(cot_g[member(s), :], fw[1])

    hidden_bias = jnp.concatenate([inbs[0][0:1], inbs[1][0:1]], axis=1)
    small[...] = jnp.zeros_like(small)

    def hidden(s):
        pre = matmul(second_g[member(s), :], fw[0]) + hidden_bias
        value, slope = gelu_pair(pre)
        act[member(s), :] = value.astype(bf16)
        grad = hb[member(s), :] * slope
        total = jnp.sum(grad, axis=0, keepdims=True)
        if s == 0:
            hsum[...] = jnp.broadcast_to(total, hsum.shape)
        else:
            hsum[...] += total
        hh[member(s), :] = grad.astype(bf16)

    group = {}

    def share(n, s, value):
        if s % 2 == 0:
            shares[n, s // 2] = value
            return
        share_out[n, s // 2] = value.astype(bf16)
        group[n, s] = link(share_out.at[n, s // 2], share_in.at[n, s // 2], partner)

    def share_near(n):
        group[n, 3].wait_recv()
        share_out[n, 2] = (shares[n, 1] + share_in[n, 1].astype(f32)).astype(bf16)
        group[n, 4] = link(share_out.at[n, 2], share_in.at[n, 2], near)

    def share_total(n):
        group[n, 1].wait_recv()
        group[n, 4].wait_recv()
        return shares[n, 0] + share_in[n, 0].astype(f32) + share_in[n, 2].astype(f32)

    w_forward(1, 0)
    w_wait(1, 1)
    back(0)
    back(1)
    w_wait(1, 0)
    hidden(0)
    share(0, 0, contract_cols(hh[member(0), :], fw[0]))
    s_pair.wait_recv()
    hidden(1)
    share(0, 1, contract_cols(hh[member(1), :], fw[0]))
    back(2)
    s_near.wait_recv()
    s_pair2 = link(second_g.at[pl.ds(2 * T, T)], second_g.at[pl.ds(3 * T, T)], partner)
    hidden(2)
    share(0, 2, contract_cols(hh[member(2), :], fw[0]))
    cot_pair2.wait_recv()
    back(3)
    s_pair2.wait_recv()
    hidden(3)
    share(0, 3, contract_cols(hh[member(3), :], fw[0]))
    share_near(0)
    h_far = link(hsum.at[:, pl.ds(half, half)], hrecv, far)

    step = 128

    def grad_rows(w, left, right):
        def chunk(c, carry):
            pw[w, blk(c, step), :] = contract_rows(left[:, blk(c, step)], right[...]).astype(bf16)
            return carry

        lax.fori_loop(0, D // step, chunk, 0)

    wg = {}

    def w_grads(part, w, n=1):
        cols = pl.ds(part * half, half)
        for k in (1, 2, 3):
            wg[part, w, k] = link(
                pw.at[pl.ds(w, n), chip_rows(k), cols],
                rw.at[part, k - 1, pl.ds(w, n)],
                along[k],
            )

    def w_sum(part, w):
        for k in (1, 2, 3):
            wg[part, w, k].wait_recv()
        total = pw[w, chip_rows(0), part * half : (part + 1) * half].astype(f32)
        for k in range(3):
            total = total + rw[part, k, w].astype(f32)
        return total

    wz_in = {}

    def w_cross(w):
        wz[w] = w_sum(1, w).astype(bf16)
        wz_in[w] = link(wz.at[w], wzr.at[w], far)

    grad_rows(0, second_g, hh)
    w_grads(1, 0)
    grad_rows(1, cot_g, act)
    w_grads(1, 1)
    second_grad = share_total(0)
    cotangent = cot_ref[...].astype(f32)
    middle_grad = cotangent + normalize_back(second_grad, norm2[...], inv_second, gains_ref[1:2])
    mgrad[...] = middle_grad
    middle_half = middle_grad.astype(bf16)
    midb[...] = middle_half
    c2a = slot(2 * nt)
    slabs = matmul(middle_half, fo[...]).astype(bf16)
    for j in range(nt):
        slab = slabs[:, j * E : (j + 1) * E]

        @pl.when(t == j)
        def _():
            cg[blk(t), :] = slab

        @pl.when(t != j)
        def _():
            cgs[j] = slab
            remote(
                cgs.at[j], cg.at[blk(t)], ss.at[c2a + j], rs.at[c2a + t], {"tensor": j}
            ).start()

    po[...] = contract_rows(midb[...], call[...]).astype(bf16)
    og = [link(po.at[core_rows(k, 1 - core)], ao.at[k], partner) for k in range(4)]
    w_grads(0, 0)
    w_grads(0, 1)
    small[1:2, :] = jnp.sum(second_grad * norm2[...], axis=0, keepdims=True)
    small[3:4, :] = jnp.sum(second_grad, axis=0, keepdims=True)
    small[4:5, :] = jnp.sum(middle_grad, axis=0, keepdims=True)
    small[5:6, :] = jnp.sum(cotangent, axis=0, keepdims=True)
    for s in (3, 1, 2, 0):
        share(1, s, contract_cols(act[member(s), :], fw[1]))
    share_near(1)

    w_cross(0)
    for k in range(1, nt):
        src = other(k)
        remote(cg.at[blk(src)], cg.at[blk(src)], ss.at[c2a], rs.at[c2a + src], far).wait_recv()

    w_cross(1)
    r2a = slot(2 * nt)
    fp = slot(nt)
    outer = (t == 0) | (t == nt - 1)
    mate = t + 1 - 2 * lax.rem(t, 2)
    inner_far = 2 - t // 2

    def crosses(b):
        return t // 2 != b // 2

    def first_pass(b):
        @pl.when(crosses(b) & jnp.logical_not(outer))
        def _():
            piece = fpass.at[b % 2]
            remote(piece, piece, ss.at[fp + b], rs.at[fp + b], near).wait_recv()
            fsend[b] = (fhold[b % 2] + fpass[b % 2].astype(f32)).astype(bf16)
            remote(
                fsend.at[b], frecv.at[t], ss.at[r2a + b], rs.at[r2a + t], {"tensor": b}
            ).start()

    og2 = {}
    for b in reversed(range(nt)):
        low = max(0, b - reach)
        width = (b + 1 - low) * T
        here, window = slice(b * T, (b + 1) * T), slice(low * T, (b + 1) * T)
        query_parts = []
        for h in range(heads):
            cols = slice(h * HEAD, (h + 1) * HEAD)
            prob = probs[h, b, :, :width]
            grad = cg[here, cols]
            prob_grad = contract_cols(grad, vs[window, cols])
            row_dot = jnp.sum(
                grad.astype(f32) * ctx[here, cols].astype(f32), axis=-1, keepdims=True
            )
            score_grad = (prob * (prob_grad - row_dot) * inv_root).astype(bf16)
            query_grad = matmul(score_grad, ks[window, cols])
            query_parts.append(query_grad)
            key_part = contract_rows(score_grad, qs[here, cols])
            value_part = contract_rows(prob.astype(bf16), grad)
            for j in range(low, b + 1):
                at = slice((j - low) * T, (j - low + 1) * T)
                to = slice(j * T, (j + 1) * T)
                if b == min(j + reach, nt - 1):
                    kacc[h, to, :] = key_part[at]
                    vacc[h, to, :] = value_part[at]
                else:
                    kacc[h, to, :] += key_part[at]
                    vacc[h, to, :] += value_part[at]
        query_rows = jnp.concatenate(query_parts, axis=1)
        value_rows = jnp.concatenate([vacc[h, here, :] for h in range(heads)], axis=1)
        key_rows = jnp.concatenate([kacc[h, here, :] for h in range(heads)], axis=1)
        block = jnp.concatenate([query_rows, key_rows, value_rows], axis=1).astype(bf16)
        ph[here, :] = block
        small[9:10, :E] += jnp.sum(query_rows, axis=0, keepdims=True)
        small[10:11, :E] += jnp.sum(value_rows, axis=0, keepdims=True)
        first_share = contract_cols(block, fq[...])

        @pl.when(t == b)
        def _():
            fown[...] = first_share

        @pl.when((t // 2 == b // 2) & (t != b))
        def _():
            fsend[b] = first_share.astype(bf16)
            remote(fsend.at[b], frecv.at[t], ss.at[r2a + b], rs.at[r2a + t], near).start()

        @pl.when(crosses(b) & outer)
        def _():
            fsend[b] = first_share.astype(bf16)
            remote(
                fsend.at[b], fpass.at[b % 2], ss.at[fp + b], rs.at[fp + b], near
            ).start()

        @pl.when(crosses(b) & jnp.logical_not(outer))
        def _():
            fhold[b % 2] = first_share

        if b == 1:
            first_pass(3)
        if b == 0:
            first_pass(2)

        if b == nt - 1:
            for k in (1, 2, 3, 0):
                og[k].wait_recv()
                total = po[core_rows(k, core), :].astype(f32) + ao[k].astype(f32)
                if k:
                    bo[k - 1] = total.astype(bf16)
                    og2[k] = link(bo.at[k - 1], ro.at[k - 1], along[k])
                else:
                    ozw[...] = total
        if b == nt - 2:
            h_far.wait_recv()
            small[8:9, mine] = hsum[0:1, :half] + hrecv[0:1]

    def chunk(c, carry):
        pq[blk(c, step), :] = contract_rows(first_ref[:, blk(c, step)], ph[...]).astype(bf16)
        return carry

    lax.fori_loop(0, D // step, chunk, 0)
    qg = [link(pq.at[core_rows(k, 1 - core)], aq.at[k], partner) for k in (0, 1, 2, 3)]
    first_pass(1)
    qg2 = {}
    for k in (1, 2, 3, 0):
        qg[k].wait_recv()
        total = pq[core_rows(k, core), :].astype(f32) + aq[k].astype(f32)
        if k:
            bq[k - 1] = total.astype(bf16)
            qg2[k] = link(bq.at[k - 1], rq.at[k - 1], along[k])
        else:
            oq[...] = total
    first_pass(0)

    out_total = ozw[...]
    for k in (1, 2, 3):
        og2[k].wait_recv()
        out_total = out_total + ro[k - 1].astype(f32)
    for j in range(nt):
        oz[j] = out_total[:, j * E : (j + 1) * E]
        ozs[j] = oz[j].astype(bf16)
    z2a = slot(2 * nt)
    for k in range(1, nt):
        copy = remote(
            ozs.at[other(k)], ozt.at[t], ss.at[z2a + k], rs.at[z2a + t], {"tensor": other(k)}
        )
        copy.start()
        sent.append(copy)

    bo_ref[...] = (mid[...] + share_total(1) + biases_ref[3:4]).astype(bf16)
    wx_in = []
    for w in (0, 1):
        own_sum = w_sum(0, w)
        wz_in[w].wait_recv()
        wsum[w] = own_sum + wzr[w].astype(f32)
        wx_in.append(link(wsum.at[w, blk(1 - core, rows), :], wx.at[w], partner))

    first_grad = fown[...]
    for src in (mate, inner_far):
        remote(frecv.at[src], frecv.at[src], ss.at[r2a], rs.at[r2a + src], far).wait_recv()
        first_grad = first_grad + frecv[src].astype(f32)
    ig_ref[...] = mgrad[...] + normalize_back(first_grad, norm1[...], inv_first, gains_ref[0:1])
    small[0:1, :] = jnp.sum(first_grad * norm1[...], axis=0, keepdims=True)
    small[2:3, :] = jnp.sum(first_grad, axis=0, keepdims=True)
    zsmall[t] = small[0:8, :]
    zin = [link(zsmall.at[t], zsmall.at[t], {"tensor": other(k)}) for k in range(1, nt)]

    out_total = oz[t]
    for k in range(1, nt):
        src = other(k)
        remote(ozt.at[src], ozt.at[src], ss.at[z2a], rs.at[z2a + src], far).wait_recv()
        out_total = out_total + ozt[src].astype(f32)
    go_ref[...] = jnp.transpose(out_total)

    for copy in zin:
        copy.wait_recv()
    summed = zsmall[0]
    for k in range(1, nt):
        summed = summed + zsmall[k]
    psmall[core] = jnp.concatenate([summed, small[8:16, :]], axis=0)
    pin = link(psmall.at[core], psmall.at[core], partner)
    total = oq[...]
    for k in (1, 2, 3):
        qg2[k].wait_recv()
        total = total + rq[k - 1].astype(f32)
    for c in range(3):
        gq_ref[c] = total[:, c * E : (c + 1) * E]
    pin.wait_recv()
    csmall[chip] = psmall[0] + psmall[1]
    cin = [link(csmall.at[chip], csmall.at[chip], along[k]) for k in (1, 2, 3)]
    for copy in wx_in:
        copy.wait_recv()
    for w, ref in ((0, gi_ref), (1, gb_ref)):
        ref[:, mine] = wsum[w, blk(core, rows), :]
        ref[:, theirs] = wx[w]
    for copy in cin:
        copy.wait_recv()
    total = csmall[0]
    for c in range(1, nc):
        total = total + csmall[c]
    gqv_ref[...] = total[9:11, :E]
    ginb_ref[...] = total[8:9, :F]
    ggain_ref[...] = total[0:2]
    gbias_ref[...] = total[2:6]
    gather_drain(0, first_ref)
    for base, piece in ((a2a, ctx.at[pl.ds(0, T)]), (c2a, cgs.at[0])):
        for b in range(nt):

            @pl.when(t != b)
            def _():
                remote(piece, piece, ss.at[base + b], rs.at[base + b], far).wait_send()

    for b in range(nt):
        piece = fsend.at[b]

        @pl.when((t != b) & jnp.logical_not(crosses(b) & outer))
        def _():
            remote(piece, piece, ss.at[r2a + b], rs.at[r2a + b], far).wait_send()

        @pl.when(crosses(b) & outer)
        def _():
            remote(piece, piece, ss.at[fp + b], rs.at[fp + b], near).wait_send()

    for copy in sent:
        copy.wait_send()


def hand_over(*refs):
    n = (len(refs) - 2) // 3
    held, sems = refs[2 * n : 3 * n], refs[3 * n :]
    loads = [pltpu.make_async_copy(refs[i], held[i], sems[0].at[i]) for i in range(n)]
    stores = [pltpu.make_async_copy(held[i], refs[n + i], sems[1].at[i]) for i in range(n)]
    for copy in loads:
        copy.start()
    for load, store in zip(loads, stores):
        load.wait()
        store.start()
    for copy in stores:
        copy.wait()


def kernel_shards(
    nt,
    nd,
    block_input,
    segment_ids,
    w_qkv,
    w_out,
    w_in,
    w_back,
    qv_bias,
    in_bias,
    norm_gains,
    norm_biases,
    out_cotangent,
):
    bf16, f32 = jnp.bfloat16, jnp.float32
    T, D = block_input.shape[1:]
    E, F = w_qkv.shape[2], w_in.shape[1]
    rows = D // nd
    seq = nt * T
    heads = E // HEAD
    nc = nd // 2
    half = F // 2
    reach = (seq // 2 - 1 + T - 1) // T
    window = min(nt, reach + 1) * T
    group = 4 * T
    vm = pltpu.VMEM
    scratch = [
        vm((D, 3 * E), bf16),
        vm((D, nt * E), bf16),
        vm((nt, rows, E), bf16),
        vm((2, D, F), bf16),
        vm((seq, D), bf16),
        vm((group, D), bf16),
        vm((group, D), bf16),
        vm((T, D), bf16),
        vm((nt, 8, T), jnp.int32),
        vm((seq, E), bf16),
        vm((seq, E), bf16),
        vm((seq, E), bf16),
        vm((seq, E), bf16),
        vm((nt, T, E), bf16),
        vm((T, nt * E), bf16),
        vm((nt, T, E), bf16),
        vm((seq, E), bf16),
        vm((heads, nt, T, window), f32),
        vm((group, F), f32),
        vm((group, F), bf16),
        vm((group, F), bf16),
        vm((seq, 3 * E), bf16),
        vm((heads, seq, HEAD), f32),
        vm((heads, seq, HEAD), f32),
        vm((nt, T, D), bf16),
        vm((nt, T, D), bf16),
        vm((2, 2, T, D), f32),
        vm((2, 3, T, D), bf16),
        vm((2, 3, T, D), bf16),
        vm((T, D), f32),
        vm((T, D), f32),
        vm((T, D), f32),
        vm((T, D), f32),
        vm((T, D), f32),
        vm((2, T, D), bf16),
        vm((2, T, D), f32),
        vm((2, D, F), bf16),
        vm((2, 3, 2, 2 * rows, half), bf16),
        vm((2, 2 * rows, half), bf16),
        vm((2, 2 * rows, half), bf16),
        vm((2, 2 * rows, half), f32),
        vm((2, rows, half), f32),
        vm((D, 3 * E), bf16),
        vm((nc, rows, 3 * E), bf16),
        vm((nc - 1, rows, 3 * E), bf16),
        vm((nc - 1, rows, 3 * E), bf16),
        vm((rows, 3 * E), f32),
        vm((D, nt * E), bf16),
        vm((nc, rows, nt * E), bf16),
        vm((nc - 1, rows, nt * E), bf16),
        vm((nc - 1, rows, nt * E), bf16),
        vm((rows, nt * E), f32),
        vm((nt, rows, E), f32),
        vm((nt, rows, E), bf16),
        vm((nt, rows, E), bf16),
        vm((2, 8, half), f32),
        vm((8, F), f32),
        vm((8, half), f32),
        vm((16, D), f32),
        vm((nt, 8, D), f32),
        vm((2, 16, D), f32),
        vm((nc, 16, D), f32),
        pltpu.SemaphoreType.DMA((1, 2 * nt)),
        pltpu.SemaphoreType.DMA((1, 2 * nt)),
        pltpu.SemaphoreType.DMA((128,)),
        pltpu.SemaphoreType.DMA((128,)),
    ]
    spec = pl.BlockSpec(memory_space=pltpu.VMEM)
    outs = pl.pallas_call(
        functools.partial(layer_kernel, nt, nd),
        out_shape=[
            jax.ShapeDtypeStruct((T, D), bf16),
            jax.ShapeDtypeStruct((T, D), f32),
            jax.ShapeDtypeStruct((3, rows, E), f32),
            jax.ShapeDtypeStruct((E, rows), f32),
            jax.ShapeDtypeStruct((rows, F), f32),
            jax.ShapeDtypeStruct((rows, F), f32),
            jax.ShapeDtypeStruct((2, E), f32),
            jax.ShapeDtypeStruct((1, F), f32),
            jax.ShapeDtypeStruct((2, D), f32),
            jax.ShapeDtypeStruct((4, D), f32),
        ],
        in_specs=[spec] * 11,
        out_specs=[spec] * 10,
        scratch_shapes=scratch,
        compiler_params=pltpu.CompilerParams(
            collective_id=0, has_side_effects=True, vmem_limit_bytes=60 * 1024 * 1024
        ),
        name="layer",
    )(
        block_input[0],
        segment_ids,
        w_qkv,
        w_out,
        w_in,
        w_back.T,
        out_cotangent[0],
        qv_bias,
        in_bias[None],
        norm_gains,
        norm_biases,
    )
    outs = pl.pallas_call(
        hand_over,
        out_shape=[jax.ShapeDtypeStruct(a.shape, a.dtype) for a in outs],
        in_specs=[pl.BlockSpec(memory_space=pl.ANY)] * 10,
        out_specs=[pl.BlockSpec(memory_space=pl.ANY)] * 10,
        scratch_shapes=[vm(a.shape, a.dtype) for a in outs]
        + [pltpu.SemaphoreType.DMA((10,))] * 2,
        name="hand_over",
    )(*outs)
    block_out, input_grad, gq, go, gi, gb, gqv, ginb, ggain, gbias = outs
    return (block_out[None], input_grad[None], gq, go, gi, gb.T, gqv, ginb[0], ggain, gbias)


def solution(mesh):
    in_specs = (
        P("dp", "tensor", None),
        P("dp", "tensor"),
        P(None, "dp", "tensor"),
        P("tensor", "dp"),
        P("dp", "tensor"),
        P("tensor", "dp"),
        P(None, "tensor"),
        P("tensor"),
        P(),
        P(),
        P("dp", "tensor", None),
    )
    out_specs = (
        P("dp", "tensor", None),
        P("dp", "tensor", None),
        P(None, "dp", "tensor"),
        P("tensor", "dp"),
        P("dp", "tensor"),
        P("tensor", "dp"),
        P(None, "tensor"),
        P("tensor"),
        P(),
        P(),
    )
    nt, nd = mesh.shape["tensor"], mesh.shape["dp"]

    def body(*args):
        block_input, w_qkv, w_in = args[0], args[2], args[4]
        tokens, features = block_input.shape[1:]
        fits = (
            nt == 4
            and nd == 2 * nt
            and w_in.shape[0] % 16 == 0
            and w_in.shape[1] % 256 == 0
            and tokens % 128 == 0
            and features % 128 == 0
            and w_in.shape[1] <= features
            and w_qkv.shape[2] % HEAD == 0
        )
        if fits:
            return kernel_shards(nt, nd, *args)
        return shards(*args)

    return jax.shard_map(body, mesh=mesh, in_specs=in_specs, out_specs=out_specs, check_vma=False)
```

```python
import functools
import math

import jax
import jax.numpy as jnp
from jax import lax
from jax.experimental import pallas as pl
from jax.experimental.pallas import tpu as pltpu
from jax.sharding import PartitionSpec as P

HEAD = 64


EPS = 1e-05
GELU_C = math.sqrt(2.0 / math.pi)
GELU_A = 0.044715


def normalize(residual, gain_row, offset_row):
    centered = residual - jnp.mean(residual, axis=-1, keepdims=True)
    inv_std = lax.rsqrt(jnp.mean(centered * centered, axis=-1, keepdims=True) + EPS)
    normed = centered * inv_std
    return (normed * gain_row + offset_row, normed, inv_std)


def normalize_back(upstream, normed, inv_std, gain_row):
    scaled = upstream * gain_row
    return inv_std * (
        scaled
        - jnp.mean(scaled, axis=-1, keepdims=True)
        - normed * jnp.mean(scaled * normed, axis=-1, keepdims=True)
    )


def gelu_pair(inputs):
    inner_arg = GELU_C * (inputs + GELU_A * inputs * inputs * inputs)
    tangent_h = jnp.tanh(inner_arg)
    value_out = 0.5 * inputs * (1.0 + tangent_h)
    slope_out = 0.5 * (1.0 + tangent_h) + 0.5 * inputs * (1.0 - tangent_h * tangent_h) * GELU_C * (
        1.0 + 3.0 * GELU_A * inputs * inputs
    )
    return (value_out, slope_out)


def contract_rows(left, right):
    return lax.dot_general(
        left, right, (((0,), (0,)), ((), ())), preferred_element_type=jnp.float32
    )


def contract_cols(left, right):
    return lax.dot_general(
        left, right, (((1,), (1,)), ((), ())), preferred_element_type=jnp.float32
    )


def masked_scores(query_block, key_rows, segment, key_end, num_heads):
    block_rows = query_block.shape[0]
    width = query_block.shape[1] // num_heads
    query_heads = query_block.reshape(block_rows, num_heads, width)
    key_heads = key_rows.reshape(key_end, num_heads, width)
    raw_scores = jnp.einsum(
        "qhd,khd->hqk", query_heads, key_heads, preferred_element_type=jnp.float32
    ) * (1.0 / math.sqrt(width))
    query_pos = jnp.arange(block_rows, dtype=jnp.int32)
    key_pos = jnp.arange(key_end, dtype=jnp.int32)
    allowed = (key_pos[None, :] <= query_pos[:, None]) & (segment[None, :] == segment[:, None])
    return jnp.where(allowed[None], raw_scores, -jnp.inf)


def attend_forward(queries, key_rows, values, segment, num_heads):
    total_rows = queries.shape[0]
    block_rows = min(512, total_rows)
    width = queries.shape[1] // num_heads
    scores = masked_scores(queries, key_rows, segment, block_rows, num_heads)
    row_max = jnp.max(scores, axis=-1, keepdims=True)
    log_total = row_max + jnp.log(jnp.sum(jnp.exp(scores - row_max), axis=-1, keepdims=True))
    weights = jnp.exp(scores - log_total).astype(jnp.bfloat16)
    value_heads = values.reshape(block_rows, num_heads, width)
    context = jnp.einsum("hqk,khd->qhd", weights, value_heads, preferred_element_type=jnp.float32)
    contexts = context.reshape(block_rows, num_heads * width).astype(jnp.bfloat16)
    return (contexts, log_total)


def attend_backward(
    queries, key_rows, values, segment, context, log_total, context_grad, num_heads
):
    total_rows = queries.shape[0]
    block_rows = min(512, total_rows)
    width = queries.shape[1] // num_heads
    inv_root = 1.0 / math.sqrt(width)
    key_grad = jnp.zeros((total_rows, num_heads, width), jnp.float32)
    value_grad = jnp.zeros((total_rows, num_heads, width), jnp.float32)
    scores = masked_scores(queries, key_rows, segment, block_rows, num_heads)
    probs = jnp.exp(scores - log_total)
    probs_half = probs.astype(jnp.bfloat16)
    grad_heads = context_grad.reshape(block_rows, num_heads, width)
    context_heads = context.reshape(block_rows, num_heads, width)
    value_heads = values.reshape(block_rows, num_heads, width)
    key_heads = key_rows.reshape(block_rows, num_heads, width)
    query_heads = queries.reshape(block_rows, num_heads, width)
    prob_grad = jnp.einsum(
        "qhd,khd->hqk", grad_heads, value_heads, preferred_element_type=jnp.float32
    )
    row_dot = jnp.transpose(
        jnp.sum(grad_heads.astype(jnp.float32) * context_heads.astype(jnp.float32), axis=-1)
    )[:, :, None]
    score_grad = (probs * (prob_grad - row_dot) * inv_root).astype(jnp.bfloat16)
    query_grads = jnp.einsum(
        "hqk,khd->qhd", score_grad, key_heads, preferred_element_type=jnp.float32
    ).reshape(block_rows, num_heads * width)
    key_grad = key_grad.at[:block_rows].add(
        jnp.einsum("hqk,qhd->khd", score_grad, query_heads, preferred_element_type=jnp.float32)
    )
    value_grad = value_grad.at[:block_rows].add(
        jnp.einsum("hqk,qhd->khd", probs_half, grad_heads, preferred_element_type=jnp.float32)
    )
    return (
        query_grads,
        key_grad.reshape(total_rows, num_heads * width),
        value_grad.reshape(total_rows, num_heads * width),
    )


def half_scatter(share):
    return lax.psum_scatter(
        share.astype(jnp.bfloat16), "tensor", scatter_dimension=0, tiled=True
    ).astype(jnp.float32)


def shards(
    block_input,
    segment_ids,
    w_qkv,
    w_out,
    w_in,
    w_back,
    qv_bias,
    in_bias,
    norm_gains,
    norm_biases,
    out_cotangent,
):
    bf16 = jnp.bfloat16
    residual = block_input[0].astype(jnp.float32)
    head_cols = w_qkv.shape[2]
    hidden_cols = w_in.shape[1]
    local_heads = head_cols // HEAD
    cuts = [head_cols, 2 * head_cols, 3 * head_cols, 4 * head_cols, 4 * head_cols + hidden_cols]
    packed = jnp.concatenate([w_qkv[0], w_qkv[1], w_qkv[2], w_out.T, w_in, w_back.T], axis=1)
    full = lax.all_gather(packed, "dp", axis=0, tiled=True)
    qkv_full = full[:, : cuts[2]]
    out_full = full[:, cuts[2] : cuts[3]]
    in_full = full[:, cuts[3] : cuts[4]]
    back_full = full[:, cuts[4] :]
    first_out, normed_first, inv_first = normalize(residual, norm_gains[0], norm_biases[0])
    first_half, segment, cotangent_full = (
        lax.all_gather(first_out.astype(bf16), "tensor", axis=0, tiled=True),
        lax.all_gather(segment_ids[0], "tensor", axis=0, tiled=True),
        lax.all_gather(out_cotangent[0], "tensor", axis=0, tiled=True),
    )
    projected = jnp.dot(first_half, qkv_full, preferred_element_type=jnp.float32)
    queries = (projected[:, : cuts[0]] + qv_bias[0]).astype(bf16)
    key_rows = projected[:, cuts[0] : cuts[1]].astype(bf16)
    values = (projected[:, cuts[1] :] + qv_bias[1]).astype(bf16)
    context, log_total = attend_forward(queries, key_rows, values, segment, local_heads)
    attn_share = half_scatter(contract_cols(context, out_full))
    middle = residual + attn_share + norm_biases[2]
    second_out, normed_second, inv_second = normalize(middle, norm_gains[1], norm_biases[1])
    second_half = lax.all_gather(second_out.astype(bf16), "tensor", axis=0, tiled=True)
    hidden_pre = jnp.dot(second_half, in_full, preferred_element_type=jnp.float32) + in_bias
    gelu_value, gelu_slope = gelu_pair(hidden_pre)
    activation = gelu_value.astype(bf16)
    mlp_share = half_scatter(contract_cols(activation, back_full))
    block_out = (middle + mlp_share + norm_biases[3]).astype(bf16)
    cotangent = out_cotangent[0].astype(jnp.float32)
    grad_back_part = contract_rows(cotangent_full, activation)
    hidden_grad = jnp.dot(cotangent_full, back_full, preferred_element_type=jnp.float32) * gelu_slope
    hidden_half = hidden_grad.astype(bf16)
    grad_in_part = contract_rows(second_half, hidden_half)
    second_grad = half_scatter(contract_cols(hidden_half, in_full))
    middle_grad = cotangent + normalize_back(second_grad, normed_second, inv_second, norm_gains[1])
    middle_full = lax.all_gather(middle_grad.astype(bf16), "tensor", axis=0, tiled=True)
    grad_out_part = contract_rows(middle_full, context)
    context_grad = jnp.dot(middle_full, out_full, preferred_element_type=jnp.float32).astype(bf16)
    query_grad, key_grad, value_grad = attend_backward(
        queries, key_rows, values, segment, context, log_total, context_grad, local_heads
    )
    proj_half = jnp.concatenate([query_grad, key_grad, value_grad], axis=1).astype(bf16)
    grad_qkv_part = contract_rows(first_half, proj_half)
    first_grad = half_scatter(contract_cols(proj_half, qkv_full))
    input_grad = middle_grad + normalize_back(first_grad, normed_first, inv_first, norm_gains[0])
    parts = jnp.concatenate(
        [grad_qkv_part, grad_out_part, grad_in_part, grad_back_part], axis=1
    ).astype(bf16)
    grads = lax.psum_scatter(parts, "dp", scatter_dimension=0, tiled=True).astype(jnp.float32)
    grad_qkv = jnp.stack([grads[:, : cuts[0]], grads[:, cuts[0] : cuts[1]], grads[:, cuts[1] : cuts[2]]])
    grad_out = grads[:, cuts[2] : cuts[3]].T
    grad_in = grads[:, cuts[3] : cuts[4]]
    grad_back = grads[:, cuts[4] :].T
    own = jnp.concatenate(
        [jnp.sum(query_grad, axis=0), jnp.sum(value_grad, axis=0), jnp.sum(hidden_grad, axis=0)]
    )
    tensors = lax.axis_size("tensor")
    rank = lax.axis_index("tensor")
    spread = jnp.where(jnp.arange(tensors)[:, None] == rank, own[None], 0.0)
    norm_terms = jnp.stack(
        [
            jnp.sum(first_grad * normed_first, axis=0),
            jnp.sum(second_grad * normed_second, axis=0),
            jnp.sum(first_grad, axis=0),
            jnp.sum(second_grad, axis=0),
            jnp.sum(middle_grad, axis=0),
            jnp.sum(cotangent, axis=0),
        ]
    )
    total = lax.psum(
        jnp.concatenate([spread.reshape(-1), norm_terms.reshape(-1)]), ("dp", "tensor")
    )
    width = own.shape[0]
    own_total = lax.dynamic_slice(total, (rank * width,), (width,))
    norm_total = total[tensors * width :].reshape(norm_terms.shape)
    return (
        block_out[None],
        input_grad[None],
        grad_qkv,
        grad_out,
        grad_in,
        grad_back,
        own_total[: 2 * head_cols].reshape(2, head_cols),
        own_total[2 * head_cols :],
        norm_total[:2],
        norm_total[2:],
    )


def matmul(left, right):
    return jnp.dot(left, right, preferred_element_type=jnp.float32)


def layer_kernel(
    nt,
    nd,
    x_ref,
    seg_ref,
    wq_ref,
    wo_ref,
    wi_ref,
    wb_ref,
    cot_ref,
    qvb_ref,
    inb_ref,
    gains_ref,
    biases_ref,
    bo_ref,
    ig_ref,
    gq_ref,
    go_ref,
    gi_ref,
    gb_ref,
    gqv_ref,
    ginb_ref,
    ggain_ref,
    gbias_ref,
    fq,
    fo,
    own_out,
    fw,
    first_ref,
    second_g,
    cot_g,
    midb,
    segs,
    qs,
    ks,
    vs,
    ctx,
    ctx_all,
    call,
    cgs,
    cg,
    probs,
    hb,
    act,
    hh,
    ph,
    kacc,
    vacc,
    fsend,
    frecv,
    shares,
    share_out,
    share_in,
    mid,
    norm1,
    norm2,
    mgrad,
    fown,
    fpass,
    fhold,
    pw,
    rw,
    wz,
    wzr,
    wsum,
    wx,
    pq,
    aq,
    bq,
    rq,
    oq,
    po,
    ao,
    bo,
    ro,
    ozw,
    oz,
    ozs,
    ozt,
    inbs,
    hsum,
    hrecv,
    small,
    zsmall,
    psmall,
    csmall,
    gs,
    gr,
    ss,
    rs,
):
    bf16 = jnp.bfloat16
    f32 = jnp.float32
    nc = nd // 2
    t = lax.axis_index("tensor")
    d = lax.axis_index("dp")
    core = lax.rem(d, 2)
    chip = d // 2
    T, D = x_ref.shape
    rows = wi_ref.shape[0]
    E = ctx.shape[1]
    F = wi_ref.shape[1]
    half = F // 2
    heads = E // HEAD
    seq = nt * T
    cy, cx = chip // 2, lax.rem(chip, 2)
    chips = (chip, cy * 2 + 1 - cx, (1 - cy) * 2 + cx, (1 - cy) * 2 + 1 - cx)
    partner = {"dp": chip * 2 + 1 - core}
    along = [{"dp": c * 2 + core} for c in chips]
    near = {"tensor": t + 1 - 2 * lax.rem(t, 2)}
    far = {"tensor": lax.rem(t + 2, nt)}

    def remote(src, dst, ssem, rsem, where):
        return pltpu.make_async_remote_copy(
            src_ref=src,
            dst_ref=dst,
            send_sem=ssem,
            recv_sem=rsem,
            device_id=where,
            device_id_type=pl.DeviceIdType.MESH,
        )

    used = []
    sent = []

    def slot(count=1):
        used.extend([0] * count)
        return len(used) - count

    def link(src, dst, where):
        i = slot()
        copy = remote(src, dst, ss.at[i], rs.at[i], where)
        copy.start()
        sent.append(copy)
        return copy

    def link_all(piece, places):
        return [link(piece, piece, where) for where in places]

    def blk(index, size=T):
        return pl.ds(pl.multiple_of(index * size, size), size)

    def chip_rows(k):
        return blk(chips[k], 2 * rows)

    def core_rows(k, c):
        return blk(chips[k] * 2 + c, rows)

    def other(k):
        return lax.rem(t + k, nt)

    def line_copy(kind, place, ref, b, to):
        piece = ref.at[blk(b)]
        return remote(piece, piece, gs.at[kind, place], gr.at[kind, b], {"tensor": to})

    def line_own(kind, ref, act_on):
        for place, to in ((0, t + 1), (2 * nt - 1, t - 1)):

            @pl.when((to >= 0) & (to < nt))
            def _():
                act_on(line_copy(kind, place, ref, t, to))

    def line_place(s):
        sign = 2 * (s % 2) - 1
        return t + sign * ((s + 1) // 2), t - sign

    def gather_send(kind, ref):
        line_own(kind, ref, lambda copy: copy.start())

    def gather_step(kind, ref, s):
        b, to = line_place(s)

        @pl.when((b >= 0) & (b < nt))
        def _():
            remote(
                ref.at[blk(b)], ref.at[blk(b)], gs.at[kind, 0], gr.at[kind, b], {"tensor": b}
            ).wait_recv()

            @pl.when((to >= 0) & (to < nt))
            def _():
                line_copy(kind, s, ref, b, to).start()

    def gather_drain(kind, ref):
        line_own(kind, ref, lambda copy: copy.wait_send())

        for s in range(1, 2 * nt - 1):
            b, to = line_place(s)

            @pl.when((b >= 0) & (b < nt) & (to >= 0) & (to < nt))
            def _():
                line_copy(kind, s, ref, b, to).wait_send()

    barrier = pltpu.get_barrier_semaphore()
    for where in [{"tensor": other(k)} for k in range(1, nt)] + along[1:] + [partner]:
        pl.semaphore_signal(barrier, inc=1, device_id=where, device_id_type=pl.DeviceIdType.MESH)
    residual = x_ref[...].astype(f32)
    first_out, normed_first, inv_first = normalize(residual, gains_ref[0:1], biases_ref[0:1])
    norm1[...] = normed_first
    first_ref[blk(t), :] = first_out.astype(bf16)
    fq[blk(d, rows), :] = jnp.concatenate([wq_ref[0], wq_ref[1], wq_ref[2]], axis=1)
    own_out[t] = jnp.transpose(wo_ref[...].astype(f32)).astype(bf16)
    mine, theirs = blk(core, half), blk(1 - core, half)
    fw[0, blk(d, rows), :half] = wi_ref[:, mine]
    fw[1, blk(d, rows), :half] = wb_ref[:, mine]
    segs[t] = jnp.broadcast_to(seg_ref[...], segs.shape[1:])
    hsum[...] = jnp.broadcast_to(inb_ref[...][None], hsum.shape)
    inbs[0] = hsum[:, mine]
    pl.semaphore_wait(barrier, nt - 1 + nc - 1 + 1)

    gather_send(0, first_ref)
    own_rows = blk(d, rows)
    lines = [{"tensor": other(k)} for k in range(1, nt)]
    q_piece = fq.at[own_rows]
    q_in = link_all(q_piece, along[1:])
    w_pair = [
        link(ref.at[:, theirs], fw.at[w, own_rows, pl.ds(0, half)], partner)
        for w, ref in ((0, wi_ref), (1, wb_ref))
    ]
    q_pair = link_all(q_piece, [partner])
    seg_in = link_all(segs.at[t], lines)
    cot_pair = link(cot_ref, cot_g.at[pl.ds(T, T)], partner)
    cot_g[0:T] = cot_ref[...]

    w_in = {}

    def w_send(part, w, n=1):
        piece = fw.at[pl.ds(w, n), chip_rows(0), pl.ds(part * half, half)]
        w_in[part, w, 1], w_in[part, w, 2] = link_all(piece, along[1:3])

    def w_forward(part, w, n=1):
        cols = pl.ds(part * half, half)
        w_in[part, w, 1].wait_recv()
        piece = fw.at[pl.ds(w, n), core_rows(1, 0), cols]
        w_in[part, w, 3] = link(piece, piece, along[2])
        w_in[part, w, 2].wait_recv()
        piece = fw.at[pl.ds(w, n), core_rows(2, 1), cols]
        w_in[part, w, 4] = link(piece, piece, along[1])

    def w_wait(part, w):
        w_in[part, w, 3].wait_recv()
        w_in[part, w, 4].wait_recv()

    for copy in w_pair:
        copy.wait_recv()
    w_send(0, 0, 2)
    w_far = [
        link(
            fw.at[w, chip_rows(0), pl.ds(0, half)], fw.at[w, chip_rows(0), pl.ds(half, half)], far
        )
        for w in (1, 0)
    ]
    inb_far = link(inbs.at[0], inbs.at[1], far)
    gather_step(0, first_ref, 1)
    gather_step(0, first_ref, 2)
    o_line = [link(own_out.at[t], own_out.at[t], where) for where in lines]
    for k in (1, 2, 3):
        q_in[k - 1].wait_recv()
        q_pair += link_all(fq.at[core_rows(k, core)], [partner])
    gather_step(0, first_ref, 3)
    gather_step(0, first_ref, 4)
    for copy in o_line:
        copy.wait_recv()
    fo[own_rows, :] = jnp.concatenate([own_out[j] for j in range(nt)], axis=1)
    o_pair = link_all(fo.at[own_rows], [partner])
    o_in = link_all(fo.at[own_rows], along[1:])
    w_forward(0, 0, 2)
    for s in range(5, 2 * nt - 1):
        gather_step(0, first_ref, s)
    cot_near = link(cot_ref, cot_g.at[pl.ds(2 * T, T)], near)
    for copy in q_pair:
        copy.wait_recv()

    inv_root = 1.0 / math.sqrt(HEAD)
    projected = matmul(first_ref[...], fq[...])
    qs[...] = (projected[:, :E] + qvb_ref[0:1]).astype(bf16)
    ks[...] = projected[:, E : 2 * E].astype(bf16)
    vs[...] = (projected[:, 2 * E :] + qvb_ref[1:2]).astype(bf16)
    for copy in seg_in:
        copy.wait_recv()

    reach = (seq // 2 - 1 + T - 1) // T
    a2a = slot(2 * nt)
    for b in range(nt):
        low = max(0, b - reach)
        width = (b + 1 - low) * T
        key_seg = jnp.concatenate([segs[j][0:1].astype(f32) for j in range(low, b + 1)], axis=1)
        query_seg = jnp.transpose(jnp.broadcast_to(segs[b][0:1].astype(f32), (T, T)))[:, 0:1]
        query_pos = lax.broadcasted_iota(jnp.int32, (T, width), 0) + b * T
        key_pos = lax.broadcasted_iota(jnp.int32, (T, width), 1) + low * T
        allowed = (key_pos <= query_pos) & (query_seg == key_seg)
        for h in range(heads):
            cols = slice(h * HEAD, (h + 1) * HEAD)
            scores = (
                contract_cols(qs[b * T : (b + 1) * T, cols], ks[low * T : (b + 1) * T, cols])
                * inv_root
            )
            scores = jnp.where(allowed, scores, -jnp.inf)
            row_max = jnp.max(scores, axis=-1, keepdims=True)
            powers = jnp.exp(scores - row_max)
            prob = powers * (1.0 / jnp.sum(powers, axis=-1, keepdims=True))
            probs[h, b, :, :width] = prob
            ctx[b * T : (b + 1) * T, cols] = matmul(
                prob.astype(bf16), vs[low * T : (b + 1) * T, cols]
            ).astype(bf16)

        @pl.when(t == b)
        def _():
            ctx_all[t] = ctx[b * T : (b + 1) * T, :]

        @pl.when(t != b)
        def _():
            remote(
                ctx.at[pl.ds(b * T, T)], ctx_all.at[t], ss.at[a2a + b], rs.at[a2a + t], {"tensor": b}
            ).start()

    for k in (1, 2, 3):
        o_in[k - 1].wait_recv()
        o_pair += link_all(fo.at[core_rows(k, core)], [partner])
    for n, w in enumerate((1, 0)):
        w_far[n].wait_recv()
        w_send(1, w)
    for k in range(1, nt):
        src = other(k)
        remote(ctx_all.at[src], ctx_all.at[src], ss.at[a2a], rs.at[a2a + src], far).wait_recv()
    call[...] = jnp.concatenate([ctx_all[j] for j in range(nt)], axis=1)
    for copy in o_pair:
        copy.wait_recv()
    middle = residual + contract_cols(call[...], fo[...]) + biases_ref[2:3]
    mid[...] = middle
    second_out, normed_second, inv_second = normalize(middle, gains_ref[1:2], biases_ref[1:2])
    norm2[...] = normed_second
    second_g[0:T] = second_out.astype(bf16)
    second_piece = second_g.at[pl.ds(0, T)]
    s_near = link(second_piece, second_g.at[pl.ds(2 * T, T)], near)
    s_pair = link(second_piece, second_g.at[pl.ds(T, T)], partner)
    w_forward(1, 1)
    w_wait(0, 0)
    inb_far.wait_recv()
    cot_near.wait_recv()
    cot_pair2 = link(cot_g.at[pl.ds(2 * T, T)], cot_g.at[pl.ds(3 * T, T)], partner)
    cot_pair.wait_recv()

    def member(s):
        return slice(s * T, (s + 1) * T)

    def back(s):
        hb[member(s), :] = matmul(cot_g[member(s), :], fw[1])

    hidden_bias = jnp.concatenate([inbs[0][0:1], inbs[1][0:1]], axis=1)
    small[...] = jnp.zeros_like(small)

    def hidden(s):
        pre = matmul(second_g[member(s), :], fw[0]) + hidden_bias
        value, slope = gelu_pair(pre)
        act[member(s), :] = value.astype(bf16)
        grad = hb[member(s), :] * slope
        total = jnp.sum(grad, axis=0, keepdims=True)
        if s == 0:
            hsum[...] = jnp.broadcast_to(total, hsum.shape)
        else:
            hsum[...] += total
        hh[member(s), :] = grad.astype(bf16)

    group = {}

    def share(n, s, value):
        if s % 2 == 0:
            shares[n, s // 2] = value
            return
        share_out[n, s // 2] = value.astype(bf16)
        group[n, s] = link(share_out.at[n, s // 2], share_in.at[n, s // 2], partner)

    def share_near(n):
        group[n, 3].wait_recv()
        share_out[n, 2] = (shares[n, 1] + share_in[n, 1].astype(f32)).astype(bf16)
        group[n, 4] = link(share_out.at[n, 2], share_in.at[n, 2], near)

    def share_total(n):
        group[n, 1].wait_recv()
        group[n, 4].wait_recv()
        return shares[n, 0] + share_in[n, 0].astype(f32) + share_in[n, 2].astype(f32)

    w_forward(1, 0)
    w_wait(1, 1)
    back(0)
    back(1)
    w_wait(1, 0)
    hidden(0)
    share(0, 0, contract_cols(hh[member(0), :], fw[0]))
    s_pair.wait_recv()
    hidden(1)
    share(0, 1, contract_cols(hh[member(1), :], fw[0]))
    back(2)
    s_near.wait_recv()
    s_pair2 = link(second_g.at[pl.ds(2 * T, T)], second_g.at[pl.ds(3 * T, T)], partner)
    hidden(2)
    share(0, 2, contract_cols(hh[member(2), :], fw[0]))
    cot_pair2.wait_recv()
    back(3)
    s_pair2.wait_recv()
    hidden(3)
    share(0, 3, contract_cols(hh[member(3), :], fw[0]))
    share_near(0)
    h_far = link(hsum.at[:, pl.ds(half, half)], hrecv, far)

    step = 128

    def grad_rows(w, left, right):
        def chunk(c, carry):
            pw[w, blk(c, step), :] = contract_rows(left[:, blk(c, step)], right[...]).astype(bf16)
            return carry

        lax.fori_loop(0, D // step, chunk, 0)

    wg = {}

    def w_grads(part, w, n=1):
        cols = pl.ds(part * half, half)
        for k in (1, 2, 3):
            wg[part, w, k] = link(
                pw.at[pl.ds(w, n), chip_rows(k), cols],
                rw.at[part, k - 1, pl.ds(w, n)],
                along[k],
            )

    def w_sum(part, w):
        for k in (1, 2, 3):
            wg[part, w, k].wait_recv()
        total = pw[w, chip_rows(0), part * half : (part + 1) * half].astype(f32)
        for k in range(3):
            total = total + rw[part, k, w].astype(f32)
        return total

    wz_in = {}

    def w_cross(w):
        wz[w] = w_sum(1, w).astype(bf16)
        wz_in[w] = link(wz.at[w], wzr.at[w], far)

    grad_rows(0, second_g, hh)
    w_grads(1, 0)
    grad_rows(1, cot_g, act)
    w_grads(1, 1)
    second_grad = share_total(0)
    cotangent = cot_ref[...].astype(f32)
    middle_grad = cotangent + normalize_back(second_grad, norm2[...], inv_second, gains_ref[1:2])
    mgrad[...] = middle_grad
    middle_half = middle_grad.astype(bf16)
    midb[...] = middle_half
    c2a = slot(2 * nt)
    slabs = matmul(middle_half, fo[...]).astype(bf16)
    for j in range(nt):
        slab = slabs[:, j * E : (j + 1) * E]

        @pl.when(t == j)
        def _():
            cg[blk(t), :] = slab

        @pl.when(t != j)
        def _():
            cgs[j] = slab
            remote(
                cgs.at[j], cg.at[blk(t)], ss.at[c2a + j], rs.at[c2a + t], {"tensor": j}
            ).start()

    po[...] = contract_rows(midb[...], call[...]).astype(bf16)
    og = [link(po.at[core_rows(k, 1 - core)], ao.at[k], partner) for k in range(4)]
    w_grads(0, 0)
    w_grads(0, 1)
    small[1:2, :] = jnp.sum(second_grad * norm2[...], axis=0, keepdims=True)
    small[3:4, :] = jnp.sum(second_grad, axis=0, keepdims=True)
    small[4:5, :] = jnp.sum(middle_grad, axis=0, keepdims=True)
    small[5:6, :] = jnp.sum(cotangent, axis=0, keepdims=True)
    for s in (3, 1, 2, 0):
        share(1, s, contract_cols(act[member(s), :], fw[1]))
    share_near(1)

    w_cross(0)
    for k in range(1, nt):
        src = other(k)
        remote(cg.at[blk(src)], cg.at[blk(src)], ss.at[c2a], rs.at[c2a + src], far).wait_recv()

    w_cross(1)
    r2a = slot(2 * nt)
    fp = slot(nt)
    outer = (t == 0) | (t == nt - 1)
    mate = t + 1 - 2 * lax.rem(t, 2)
    inner_far = 2 - t // 2

    def crosses(b):
        return t // 2 != b // 2

    def first_pass(b):
        @pl.when(crosses(b) & jnp.logical_not(outer))
        def _():
            piece = fpass.at[b % 2]
            remote(piece, piece, ss.at[fp + b], rs.at[fp + b], near).wait_recv()
            fsend[b] = (fhold[b % 2] + fpass[b % 2].astype(f32)).astype(bf16)
            remote(
                fsend.at[b], frecv.at[t], ss.at[r2a + b], rs.at[r2a + t], {"tensor": b}
            ).start()

    og2 = {}
    for b in reversed(range(nt)):
        low = max(0, b - reach)
        width = (b + 1 - low) * T
        here, window = slice(b * T, (b + 1) * T), slice(low * T, (b + 1) * T)
        query_parts = []
        for h in range(heads):
            cols = slice(h * HEAD, (h + 1) * HEAD)
            prob = probs[h, b, :, :width]
            grad = cg[here, cols]
            prob_grad = contract_cols(grad, vs[window, cols])
            row_dot = jnp.sum(
                grad.astype(f32) * ctx[here, cols].astype(f32), axis=-1, keepdims=True
            )
            score_grad = (prob * (prob_grad - row_dot) * inv_root).astype(bf16)
            query_grad = matmul(score_grad, ks[window, cols])
            query_parts.append(query_grad)
            key_part = contract_rows(score_grad, qs[here, cols])
            value_part = contract_rows(prob.astype(bf16), grad)
            for j in range(low, b + 1):
                at = slice((j - low) * T, (j - low + 1) * T)
                to = slice(j * T, (j + 1) * T)
                if b == min(j + reach, nt - 1):
                    kacc[h, to, :] = key_part[at]
                    vacc[h, to, :] = value_part[at]
                else:
                    kacc[h, to, :] += key_part[at]
                    vacc[h, to, :] += value_part[at]
        query_rows = jnp.concatenate(query_parts, axis=1)
        value_rows = jnp.concatenate([vacc[h, here, :] for h in range(heads)], axis=1)
        key_rows = jnp.concatenate([kacc[h, here, :] for h in range(heads)], axis=1)
        block = jnp.concatenate([query_rows, key_rows, value_rows], axis=1).astype(bf16)
        ph[here, :] = block
        small[9:10, :E] += jnp.sum(query_rows, axis=0, keepdims=True)
        small[10:11, :E] += jnp.sum(value_rows, axis=0, keepdims=True)
        first_share = contract_cols(block, fq[...])

        @pl.when(t == b)
        def _():
            fown[...] = first_share

        @pl.when((t // 2 == b // 2) & (t != b))
        def _():
            fsend[b] = first_share.astype(bf16)
            remote(fsend.at[b], frecv.at[t], ss.at[r2a + b], rs.at[r2a + t], near).start()

        @pl.when(crosses(b) & outer)
        def _():
            fsend[b] = first_share.astype(bf16)
            remote(
                fsend.at[b], fpass.at[b % 2], ss.at[fp + b], rs.at[fp + b], near
            ).start()

        @pl.when(crosses(b) & jnp.logical_not(outer))
        def _():
            fhold[b % 2] = first_share

        if b == 1:
            first_pass(3)
        if b == 0:
            first_pass(2)

        if b == nt - 1:
            for k in (1, 2, 3, 0):
                og[k].wait_recv()
                total = po[core_rows(k, core), :].astype(f32) + ao[k].astype(f32)
                if k:
                    bo[k - 1] = total.astype(bf16)
                    og2[k] = link(bo.at[k - 1], ro.at[k - 1], along[k])
                else:
                    ozw[...] = total
        if b == nt - 2:
            h_far.wait_recv()
            small[8:9, mine] = hsum[0:1, :half] + hrecv[0:1]

    def chunk(c, carry):
        pq[blk(c, step), :] = contract_rows(first_ref[:, blk(c, step)], ph[...]).astype(bf16)
        return carry

    lax.fori_loop(0, D // step, chunk, 0)
    qg = [link(pq.at[core_rows(k, 1 - core)], aq.at[k], partner) for k in (0, 1, 2, 3)]
    first_pass(1)
    qg2 = {}
    for k in (1, 2, 3, 0):
        qg[k].wait_recv()
        total = pq[core_rows(k, core), :].astype(f32) + aq[k].astype(f32)
        if k:
            bq[k - 1] = total.astype(bf16)
            qg2[k] = link(bq.at[k - 1], rq.at[k - 1], along[k])
        else:
            oq[...] = total
    first_pass(0)

    out_total = ozw[...]
    for k in (1, 2, 3):
        og2[k].wait_recv()
        out_total = out_total + ro[k - 1].astype(f32)
    for j in range(nt):
        oz[j] = out_total[:, j * E : (j + 1) * E]
        ozs[j] = oz[j].astype(bf16)
    z2a = slot(2 * nt)
    for k in range(1, nt):
        copy = remote(
            ozs.at[other(k)], ozt.at[t], ss.at[z2a + k], rs.at[z2a + t], {"tensor": other(k)}
        )
        copy.start()
        sent.append(copy)

    bo_ref[...] = (mid[...] + share_total(1) + biases_ref[3:4]).astype(bf16)
    wx_in = []
    for w in (0, 1):
        own_sum = w_sum(0, w)
        wz_in[w].wait_recv()
        wsum[w] = own_sum + wzr[w].astype(f32)
        wx_in.append(link(wsum.at[w, blk(1 - core, rows), :], wx.at[w], partner))

    first_grad = fown[...]
    for src in (mate, inner_far):
        remote(frecv.at[src], frecv.at[src], ss.at[r2a], rs.at[r2a + src], far).wait_recv()
        first_grad = first_grad + frecv[src].astype(f32)
    ig_ref[...] = mgrad[...] + normalize_back(first_grad, norm1[...], inv_first, gains_ref[0:1])
    small[0:1, :] = jnp.sum(first_grad * norm1[...], axis=0, keepdims=True)
    small[2:3, :] = jnp.sum(first_grad, axis=0, keepdims=True)
    zsmall[t] = small[0:8, :]
    zin = [link(zsmall.at[t], zsmall.at[t], {"tensor": other(k)}) for k in range(1, nt)]

    out_total = oz[t]
    for k in range(1, nt):
        src = other(k)
        remote(ozt.at[src], ozt.at[src], ss.at[z2a], rs.at[z2a + src], far).wait_recv()
        out_total = out_total + ozt[src].astype(f32)
    go_ref[...] = jnp.transpose(out_total)

    for copy in zin:
        copy.wait_recv()
    summed = zsmall[0]
    for k in range(1, nt):
        summed = summed + zsmall[k]
    psmall[core] = jnp.concatenate([summed, small[8:16, :]], axis=0)
    pin = link(psmall.at[core], psmall.at[core], partner)
    total = oq[...]
    for k in (1, 2, 3):
        qg2[k].wait_recv()
        total = total + rq[k - 1].astype(f32)
    for c in range(3):
        gq_ref[c] = total[:, c * E : (c + 1) * E]
    pin.wait_recv()
    csmall[chip] = psmall[0] + psmall[1]
    cin = [link(csmall.at[chip], csmall.at[chip], along[k]) for k in (1, 2, 3)]
    for copy in wx_in:
        copy.wait_recv()
    for w, ref in ((0, gi_ref), (1, gb_ref)):
        ref[:, mine] = wsum[w, blk(core, rows), :]
        ref[:, theirs] = wx[w]
    for copy in cin:
        copy.wait_recv()
    total = csmall[0]
    for c in range(1, nc):
        total = total + csmall[c]
    gqv_ref[...] = total[9:11, :E]
    ginb_ref[...] = total[8:9, :F]
    ggain_ref[...] = total[0:2]
    gbias_ref[...] = total[2:6]
    gather_drain(0, first_ref)
    for base, piece in ((a2a, ctx.at[pl.ds(0, T)]), (c2a, cgs.at[0])):
        for b in range(nt):

            @pl.when(t != b)
            def _():
                remote(piece, piece, ss.at[base + b], rs.at[base + b], far).wait_send()

    for b in range(nt):
        piece = fsend.at[b]

        @pl.when((t != b) & jnp.logical_not(crosses(b) & outer))
        def _():
            remote(piece, piece, ss.at[r2a + b], rs.at[r2a + b], far).wait_send()

        @pl.when(crosses(b) & outer)
        def _():
            remote(piece, piece, ss.at[fp + b], rs.at[fp + b], near).wait_send()

    for copy in sent:
        copy.wait_send()


def hand_over(*refs):
    n = (len(refs) - 2) // 3
    held, sems = refs[2 * n : 3 * n], refs[3 * n :]
    loads = [pltpu.make_async_copy(refs[i], held[i], sems[0].at[i]) for i in range(n)]
    stores = [
        pltpu.make_async_copy(held[i], refs[n + i], sems[1].at[i])
        if len(refs[n + i].shape) > 1
        else None
        for i in range(n)
    ]
    for copy in loads:
        copy.start()
    flat = [i for i in range(n) if len(refs[n + i].shape) == 1]
    for i in range(n):
        loads[i].wait()
        if i in flat:
            refs[n + i][...] = held[i][0]
        else:
            stores[i].start()
    for i in range(n):
        if i not in flat:
            stores[i].wait()


def kernel_shards(
    nt,
    nd,
    block_input,
    segment_ids,
    w_qkv,
    w_out,
    w_in,
    w_back,
    qv_bias,
    in_bias,
    norm_gains,
    norm_biases,
    out_cotangent,
):
    bf16, f32 = jnp.bfloat16, jnp.float32
    T, D = block_input.shape[1:]
    E, F = w_qkv.shape[2], w_in.shape[1]
    rows = D // nd
    seq = nt * T
    heads = E // HEAD
    nc = nd // 2
    half = F // 2
    reach = (seq // 2 - 1 + T - 1) // T
    window = min(nt, reach + 1) * T
    group = 4 * T
    vm = pltpu.VMEM
    scratch = [
        vm((D, 3 * E), bf16),
        vm((D, nt * E), bf16),
        vm((nt, rows, E), bf16),
        vm((2, D, F), bf16),
        vm((seq, D), bf16),
        vm((group, D), bf16),
        vm((group, D), bf16),
        vm((T, D), bf16),
        vm((nt, 8, T), jnp.int32),
        vm((seq, E), bf16),
        vm((seq, E), bf16),
        vm((seq, E), bf16),
        vm((seq, E), bf16),
        vm((nt, T, E), bf16),
        vm((T, nt * E), bf16),
        vm((nt, T, E), bf16),
        vm((seq, E), bf16),
        vm((heads, nt, T, window), f32),
        vm((group, F), f32),
        vm((group, F), bf16),
        vm((group, F), bf16),
        vm((seq, 3 * E), bf16),
        vm((heads, seq, HEAD), f32),
        vm((heads, seq, HEAD), f32),
        vm((nt, T, D), bf16),
        vm((nt, T, D), bf16),
        vm((2, 2, T, D), f32),
        vm((2, 3, T, D), bf16),
        vm((2, 3, T, D), bf16),
        vm((T, D), f32),
        vm((T, D), f32),
        vm((T, D), f32),
        vm((T, D), f32),
        vm((T, D), f32),
        vm((2, T, D), bf16),
        vm((2, T, D), f32),
        vm((2, D, F), bf16),
        vm((2, 3, 2, 2 * rows, half), bf16),
        vm((2, 2 * rows, half), bf16),
        vm((2, 2 * rows, half), bf16),
        vm((2, 2 * rows, half), f32),
        vm((2, rows, half), f32),
        vm((D, 3 * E), bf16),
        vm((nc, rows, 3 * E), bf16),
        vm((nc - 1, rows, 3 * E), bf16),
        vm((nc - 1, rows, 3 * E), bf16),
        vm((rows, 3 * E), f32),
        vm((D, nt * E), bf16),
        vm((nc, rows, nt * E), bf16),
        vm((nc - 1, rows, nt * E), bf16),
        vm((nc - 1, rows, nt * E), bf16),
        vm((rows, nt * E), f32),
        vm((nt, rows, E), f32),
        vm((nt, rows, E), bf16),
        vm((nt, rows, E), bf16),
        vm((2, 8, half), f32),
        vm((8, F), f32),
        vm((8, half), f32),
        vm((16, D), f32),
        vm((nt, 8, D), f32),
        vm((2, 16, D), f32),
        vm((nc, 16, D), f32),
        pltpu.SemaphoreType.DMA((1, 2 * nt)),
        pltpu.SemaphoreType.DMA((1, 2 * nt)),
        pltpu.SemaphoreType.DMA((128,)),
        pltpu.SemaphoreType.DMA((128,)),
    ]
    spec = pl.BlockSpec(memory_space=pltpu.VMEM)
    outs = pl.pallas_call(
        functools.partial(layer_kernel, nt, nd),
        out_shape=[
            jax.ShapeDtypeStruct((T, D), bf16),
            jax.ShapeDtypeStruct((T, D), f32),
            jax.ShapeDtypeStruct((3, rows, E), f32),
            jax.ShapeDtypeStruct((E, rows), f32),
            jax.ShapeDtypeStruct((rows, F), f32),
            jax.ShapeDtypeStruct((rows, F), f32),
            jax.ShapeDtypeStruct((2, E), f32),
            jax.ShapeDtypeStruct((1, F), f32),
            jax.ShapeDtypeStruct((2, D), f32),
            jax.ShapeDtypeStruct((4, D), f32),
        ],
        in_specs=[spec] * 11,
        out_specs=[spec] * 10,
        scratch_shapes=scratch,
        compiler_params=pltpu.CompilerParams(
            collective_id=0, has_side_effects=True, vmem_limit_bytes=60 * 1024 * 1024
        ),
        name="layer",
    )(
        block_input[0],
        segment_ids,
        w_qkv,
        w_out,
        w_in,
        w_back.T,
        out_cotangent[0],
        qv_bias,
        in_bias,
        norm_gains,
        norm_biases,
    )
    outs = pl.pallas_call(
        hand_over,
        out_shape=[
            jax.ShapeDtypeStruct(a.shape[1:] if a.shape[0] == 1 else a.shape, a.dtype) for a in outs
        ],
        in_specs=[pl.BlockSpec(memory_space=pl.ANY)] * 10,
        out_specs=[
            pl.BlockSpec(memory_space=pltpu.VMEM if a.shape[0] == 1 else pl.ANY) for a in outs
        ],
        scratch_shapes=[vm(a.shape, a.dtype) for a in outs]
        + [pltpu.SemaphoreType.DMA((10,))] * 2,
        name="hand_over",
    )(*outs)
    block_out, input_grad, gq, go, gi, gb, gqv, ginb, ggain, gbias = outs
    return (block_out[None], input_grad[None], gq, go, gi, gb.T, gqv, ginb, ggain, gbias)


def solution(mesh):
    in_specs = (
        P("dp", "tensor", None),
        P("dp", "tensor"),
        P(None, "dp", "tensor"),
        P("tensor", "dp"),
        P("dp", "tensor"),
        P("tensor", "dp"),
        P(None, "tensor"),
        P("tensor"),
        P(),
        P(),
        P("dp", "tensor", None),
    )
    out_specs = (
        P("dp", "tensor", None),
        P("dp", "tensor", None),
        P(None, "dp", "tensor"),
        P("tensor", "dp"),
        P("dp", "tensor"),
        P("tensor", "dp"),
        P(None, "tensor"),
        P("tensor"),
        P(),
        P(),
    )
    nt, nd = mesh.shape["tensor"], mesh.shape["dp"]

    def body(*args):
        block_input, w_qkv, w_in = args[0], args[2], args[4]
        tokens, features = block_input.shape[1:]
        fits = (
            nt == 4
            and nd == 2 * nt
            and w_in.shape[0] % 16 == 0
            and w_in.shape[1] % 256 == 0
            and tokens % 128 == 0
            and features % 128 == 0
            and w_in.shape[1] <= features
            and w_qkv.shape[2] % HEAD == 0
        )
        if fits:
            return kernel_shards(nt, nd, *args)
        return shards(*args)

    return jax.shard_map(body, mesh=mesh, in_specs=in_specs, out_specs=out_specs, check_vma=False)
```
